128 devices in a mesh: fiber: 2 (over z_lo), blk: 64 (over z_hi, x, y, core).
Axes of the slice: x: 4, y: 4, z: 4 (z_hi: 2, z_lo: 2; z = z_hi * 2 + z_lo), core: 2. Of those that a mesh axis runs over, the one named last changes fastest.
Arguments:
- users: bfloat16 [131072, 256], P('blk', 'fiber'), may hold values from -1.5 to 1.5
- items: bfloat16 [16384, 256], P('blk'), may hold values from -1.5 to 1.5
- tile_users: int32 [64, 2, 512], P('blk', 'fiber'), may hold values from 0 to 15
- tile_items: int32 [64, 2, 512], P('blk', 'fiber'), may hold values from 0 to 127, as said below
- confidence: bfloat16 [64, 2, 512, 128, 128], P('blk', 'fiber'), may hold values from 0.19921875 to 5
Outputs:
- user_grad: bfloat16 [131072, 256], P('blk', 'fiber')
The draws below stay inside these ranges and needn't reach their ends.
Inputs may be any that keep to these rules, and one draw needn't show every extreme that they name: `tile_items`: each device's list is sorted by item block, then user block, and holds distinct pairs; the two lists of the same index of blk share no pair. A device has at most 8 tiles in any item block, and exactly 8 in at least one.
All inputs are finite; a program needn't handle non-finite values.
Results may differ from the reference program's by a relative error of at most 0.0034.
Values may be sent and summed in bfloat16 or wider, within the bound.
A program may use at most 128 MiB of HBM per device.

```python
import math
import jax
import jax.numpy as jnp
from jax import lax

R = 256
TB = 128
MOST = 8
UBD = 16
NIB = 128
TILES = 512
NU = 131072
NI = 16384
N_FIBER = 2
N_BLK = 64


def tile_lists(key):
    pairs = NIB * UBD

    def one_device(device_key):
        key_perm, key_bias, key_score, key_full = jax.random.split(device_key, 4)
        orders = jax.vmap(lambda k: jax.random.permutation(k, UBD))(jax.random.split(key_perm, NIB))
        picked = orders[:, :MOST * N_FIBER].reshape(NIB, N_FIBER, MOST).transpose(1, 0, 2).astype(jnp.int32)
        bias = jax.random.randint(key_bias, (N_FIBER, NIB), 0, 2 ** 16)
        full_block = jax.random.randint(key_full, (N_FIBER,), 0, NIB)
        bias = jnp.where(jnp.arange(NIB)[None, :] == full_block[:, None], 2 ** 17, bias)
        raw = jax.random.randint(key_score, (N_FIBER, NIB, MOST), 0, 2 ** 16)
        pair_ids = jnp.arange(NIB, dtype=jnp.int32)[None, :, None] * UBD + picked
        scores = ((raw + bias[:, :, None]) * pairs + pair_ids).reshape(N_FIBER, -1).astype(jnp.int32)
        best = lax.top_k(scores, TILES)[0]
        chosen = jnp.sort(best % pairs, axis=-1).astype(jnp.int32)
        return (chosen % UBD, chosen // UBD)
    device_keys = jax.random.split(jax.random.fold_in(key, 11), N_BLK)
    return jax.vmap(one_device)(device_keys)


def draw_tile_users(key, part):
    return tile_lists(key)[0].astype(jnp.int32)


def draw_tile_items(key, part):
    return tile_lists(key)[1].astype(jnp.int32)


def levels(rng, extent, cuts, smallest, high):
    level, own = 1.0, jax.random.fold_in(rng, 6)
    for dim, shards_of in cuts:
        heights = jnp.exp(jax.random.uniform(jax.random.fold_in(own, dim), (shards_of,), jnp.float32, smallest / len(cuts), high / len(cuts)))
        level = level * jnp.repeat(heights, extent[dim] // shards_of).reshape([-1 if axis == dim else 1 for axis in range(len(extent))])
    return level


def centred(key, extent, width, most, cuts=(), kind=jnp.bfloat16):
    factor_of = levels(key, extent, cuts, -0.22, 0.18) if cuts else 1.0
    values = jax.random.normal(key, extent, jnp.float32) * width * factor_of
    return jnp.minimum(jnp.maximum(values, -most), most).astype(kind)


def setup_inputs(seed: int = 0) -> dict:
    key_of = jax.random.split(jax.random.key(seed), 6)
    users = centred(key_of[0], (NU, R), 0.25, 1.5, ((0, 64), (1, 2)))
    items = centred(key_of[1], (NI, R), 0.25, 1.5, ((0, 64),))
    tile_users = draw_tile_users(jax.random.fold_in(key_of[5], 71), 0)
    tile_items = draw_tile_items(jax.random.fold_in(key_of[5], 71), 0)
    confidence = jnp.clip(jnp.exp(math.log(5.0) - 3.2227897 * jax.random.uniform(key_of[4], (N_BLK, N_FIBER, TILES, TB, TB), jnp.float32) ** levels(key_of[4], (N_BLK, N_FIBER, TILES, TB, TB), ((0, 64), (1, 2)), -0.2, 0.2)), 0.19921875, 5.0).astype(jnp.bfloat16)
    return {"users": users, "items": items, "tile_users": tile_users, "tile_items": tile_items, "confidence": confidence}


def reference(users, items, tile_users, tile_items, confidence):
    user_blocks = users.reshape(-1, TB, R)
    item_blocks = items.reshape(-1, TB, R)
    offsets = (jnp.arange(N_BLK, dtype=jnp.int32) * UBD)[:, None, None]
    list_users = (tile_users + offsets).astype(jnp.int32).reshape(-1, TILES)
    list_items = tile_items.reshape(-1, TILES)
    conf_lists = confidence.reshape(-1, TILES, TB, TB)

    def device_step(carry, inputs):
        totals, row_weight = carry
        user_ids, item_ids, conf_tiles = inputs
        user_rows = user_blocks[user_ids].astype(jnp.float32)
        item_rows = item_blocks[item_ids].astype(jnp.float32)
        scores = jnp.einsum('tar,tbr->tab', user_rows, item_rows, precision=lax.Precision.HIGHEST)
        weight = (conf_tiles.astype(jnp.float32) * (1.0 - scores)).astype(jnp.bfloat16)
        weight = lax.optimization_barrier(weight).astype(jnp.float32)
        products = jnp.einsum('tab,tbr->tar', weight, item_rows, precision=lax.Precision.HIGHEST)
        totals = totals.at[user_ids].add(products)
        row_weight = row_weight.at[user_ids].add(lax.optimization_barrier(jnp.sum(conf_tiles.astype(jnp.float32), axis=-1)))
        return ((totals, row_weight), None)
    start = (jnp.zeros((user_blocks.shape[0], TB, R), jnp.float32), jnp.ones((user_blocks.shape[0], TB), jnp.float32))
    (totals, row_weight), _ = lax.scan(device_step, start, (list_users, list_items, conf_lists))
    scaled = totals * lax.rsqrt(row_weight)[:, :, None]
    return scaled.reshape(-1, R).astype(jnp.bfloat16)
```

```python
import functools

import jax
import jax.numpy as jnp
from jax import lax
from jax.experimental import pallas as pl
from jax.experimental.pallas import tpu as pltpu
from jax.sharding import PartitionSpec as P

MESH = pl.DeviceIdType.MESH
TB = 128
UB = 16
IB = 128
T = 512
R = 256
G = 4
SLOTS = 640


def order_tiles(tu_ref, ti_ref, perm_ref):
    users = tu_ref[...]
    owner = lax.broadcasted_iota(jnp.int32, (UB, T), 0) == users
    hot = owner.astype(jnp.float32).astype(jnp.bfloat16)
    before = lax.broadcasted_iota(jnp.int32, (T, T), 0) < lax.broadcasted_iota(jnp.int32, (T, T), 1)
    rank = jnp.dot(hot, before.astype(jnp.float32).astype(jnp.bfloat16), preferred_element_type=jnp.float32)
    count = jnp.sum(owner.astype(jnp.float32), axis=1, keepdims=True)
    steps = jnp.floor((count + (G - 1)) * (1.0 / G))
    earlier = lax.broadcasted_iota(jnp.int32, (UB, TB), 0)
    start = jnp.zeros((UB, 1), jnp.float32)
    for a in range(UB - 1):
        start = start + jnp.where(earlier[:, :1] > a, steps[a : a + 1, :] * G, 0.0)
    place = jnp.sum(jnp.where(owner, rank + start, 0.0), axis=0, keepdims=True)
    match = lax.broadcasted_iota(jnp.int32, (SLOTS, T), 0) == place.astype(jnp.int32)
    number = lax.broadcasted_iota(jnp.int32, (1, T), 1) + 1
    rows = lax.broadcasted_iota(jnp.int32, (8, T), 0)
    fields = jnp.where(
        rows == 0,
        number // 256,
        jnp.where(rows == 1, number % 256, jnp.where(rows == 2, ti_ref[...], users)),
    )
    found = lax.dot_general(
        fields.astype(jnp.float32).astype(jnp.bfloat16),
        match.astype(jnp.float32).astype(jnp.bfloat16),
        (((1,), (1,)), ((), ())),
        preferred_element_type=jnp.float32,
    )
    packed = found[0:1] * (256.0 * 2048.0) + found[1:2] * 2048.0 + found[2:3] * 16.0 + found[3:4]
    total = jnp.sum(steps, axis=0, keepdims=True)
    out_rows = lax.broadcasted_iota(jnp.int32, (8, SLOTS), 0)
    perm_ref[...] = jnp.where(out_rows == 0, packed, total).astype(jnp.int32)


def gather_kernel(users, items, conf, tu, ti, u_all, v_all, vt_all, c_all, perm, send, recv, local):
    f, b = lax.axis_index("fiber"), lax.axis_index("blk")
    zh, x, y, k = b // 32, (b // 8) % 4, (b // 2) % 4, b % 2
    p, q = x * (1 - k) + y * k, y * (1 - k) + x * k

    def shard(zh_, p_, q_, k_):
        return zh_ * 32 + (p_ * (1 - k_) + q_ * k_) * 8 + (q_ * (1 - k_) + p_ * k_) * 2 + k_

    def zr(r):
        return zh if r == 0 else 1 - zh

    def mine(r, dp, dq):
        return shard(zr(r), (p + dp) % 4, (q + dq) % 4, k)

    def others(r, dp, dq):
        return shard(zr(r), (q + dp) % 4, (p + dq) % 4, 1 - k)

    def dev(blk, fib=f):
        return {"fiber": fib, "blk": blk}

    first = {1: dev(shard(zh, (p + 1) % 4, q, k)), -1: dev(shard(zh, (p + 3) % 4, q, k))}
    second = {1: dev(shard(zh, p, (q + 1) % 4, k)), -1: dev(shard(zh, p, (q + 3) % 4, k))}
    across = dev(shard(1 - zh, p, q, k), 1 - f)
    sibling = dev(b + 1 - 2 * k)
    partner = dev(b, 1 - f)
    around = [first[1], first[-1], second[1], second[-1], across, sibling, partner]

    barrier = pltpu.get_barrier_semaphore()
    for d in around:
        pl.semaphore_signal(barrier, inc=1, device_id=d, device_id_type=MESH)
    pl.semaphore_wait(barrier, len(around))

    def slot(r, dp, dq):
        return r * 16 + (dp % 4) * 4 + dq % 4

    def block(ref, s):
        return ref.at[pl.ds(s * 2, 2)]

    def copy(src, dst, n, d):
        return pltpu.make_async_remote_copy(
            src_ref=src, dst_ref=dst, send_sem=send.at[n], recv_sem=recv.at[n], device_id=d, device_id_type=MESH
        )

    sent = []

    def push(r, dp, dq, to, d, n_dp, n_dq, n_r):
        s = mine(r, dp, dq)
        src = items if (r, dp, dq) == (0, 0, 0) else block(v_all, s)
        c = copy(src, block(v_all, s), slot(n_r, n_dp, n_dq) + to, d)
        c.start()
        sent.append(c)

    def have(r, dp, dq):
        if dp == 0 and dq == 0:
            if r == 0:
                push(r, 0, 0, 0, across, 0, 0, 1)
            push(r, 0, 0, 0, first[1], -1, 0, r)
            push(r, 0, 0, 0, first[-1], 1, 0, r)
        if dq == 0:
            if dp == -1 and r == 0:
                push(r, dp, 0, 0, first[1], -2, 0, r)
            if dp == 1 and r == 1:
                push(r, dp, 0, 0, first[-1], 2, 0, r)
            push(r, dp, 0, 0, second[1], dp, -1, r)
            push(r, dp, 0, 0, second[-1], dp, 1, r)
        if dq == -1 and r == 0:
            push(r, dp, dq, 0, second[1], dp, -2, r)
        if dq == 1 and r == 1:
            push(r, dp, dq, 0, second[-1], dp, 2, r)
        push(r, dp, dq, 32, sibling, dp, dq, r)

    def turn(s):
        for j in range(2):
            vt_all[s * 2 + j] = v_all[s * 2 + j].T

    def arrive(r, dp, dq):
        s = mine(r, dp, dq)
        copy(block(v_all, s), block(v_all, s), slot(r, dp, dq), sibling).wait_recv()
        have(r, dp, dq)
        turn(s)

    def arrive_sibling(r, dp, dq):
        s = others(r, dp, dq)
        copy(block(v_all, s), block(v_all, s), slot(r, dp, dq) + 32, sibling).wait_recv()
        turn(s)

    own = pltpu.make_async_copy(items, block(v_all, b), local.at[0])
    half = pltpu.make_async_copy(users, u_all.at[f], local.at[1])
    tiles = pltpu.make_async_copy(conf, c_all.at[pl.ds(1, T)], local.at[2])
    have(0, 0, 0)
    swap = copy(users, u_all.at[f], 64, partner)
    swap.start()
    own.start()
    half.start()
    tiles.start()
    c_all[0] = jnp.zeros((TB, TB), jnp.bfloat16)
    own.wait()

    groups = [
        [(1, 0, 0)],
        [(0, -1, 0), (0, 1, 0)],
        [(0, 0, -1), (0, 0, 1)],
        [(1, -1, 0), (1, 1, 0)],
        [(1, 0, -1), (1, 0, 1)],
        [(0, -2, 0), (1, 2, 0)],
        [(0, -1, -1), (0, -1, 1), (0, 1, -1), (0, 1, 1)],
        [(0, 0, -2), (1, 0, 2)],
        [(1, -1, -1), (1, -1, 1), (1, 1, -1), (1, 1, 1)],
        [(0, -1, -2), (1, -1, 2), (0, 1, -2), (1, 1, 2)],
        [(0, -2, -1), (0, -2, 1), (1, 2, -1), (1, 2, 1)],
        [(0, -2, -2), (1, 2, 2)],
    ]
    late = [(0, 0, 0)]
    turn(b)
    order_tiles(tu, ti, perm)
    for group in groups:
        for event in group:
            arrive(*event)
        for event in late:
            arrive_sibling(*event)
        late = group
    for event in late:
        arrive_sibling(*event)
    copy(users, u_all.at[1 - f], 64, partner).wait_recv()
    half.wait()
    tiles.wait()
    swap.wait_send()
    for c in sent:
        c.wait_send()


def products_kernel(perm, u_all, v_all, vt_all, c_all, keep_ref, give_ref, weight_ref, totals, sums):
    f = lax.axis_index("fiber")
    totals[...] = jnp.zeros_like(totals)
    sums[...] = jnp.zeros_like(sums)
    steps = perm[1, 0]

    def entry(s, j):
        return perm[0, s * G + j]

    def item(e):
        return lax.shift_right_logical(e, 4) & 127

    def rows(s):
        a = entry(s, 0) & 15
        return pl.ds(pl.multiple_of(a * TB, TB), TB)

    def scoped(a0, a1, b0, b1, p0, p1):
        even, odd, prod = (a0, a1), (b0, b1), (p0, p1)

        def issue(s, acc):
            d = rows(s)
            u = jnp.concatenate([u_all[0, d, :], u_all[1, d, :]], axis=1)
            for m in range(2):
                e0, e1 = entry(s, 2 * m), entry(s, 2 * m + 1)
                vt = jnp.concatenate([vt_all[item(e0)], vt_all[item(e1)]], axis=1)
                pltpu.matmul_push_rhs(vt, 0, m)
                pltpu.matmul_acc_lhs(acc[m], u, load_staged_rhs=0)

        def finish(s, acc):
            d = rows(s)
            entries = [entry(s, j) for j in range(G)]
            weight_sum = None
            for m in range(2):
                e0, e1 = entries[2 * m], entries[2 * m + 1]
                v = jnp.concatenate([v_all[item(e0)], v_all[item(e1)]], axis=0)
                pltpu.matmul_push_rhs(v, 1, m)
            for m in range(2):
                e0, e1 = entries[2 * m], entries[2 * m + 1]
                scores = pltpu.matmul_pop(acc[m])
                c0 = c_all[lax.shift_right_logical(e0, 11)].astype(jnp.float32)
                c1 = c_all[lax.shift_right_logical(e1, 11)].astype(jnp.float32)
                weight = jnp.concatenate([c0, c1], axis=1) * (1.0 - scores)
                pltpu.matmul_acc_lhs(prod[m], weight.astype(jnp.bfloat16), load_staged_rhs=1)
                weight_sum = c0 + c1 if weight_sum is None else weight_sum + (c0 + c1)
            sums[d, :] += weight_sum
            return d

        def flush(d):
            totals[d, :] += pltpu.matmul_pop(prod[0]) + pltpu.matmul_pop(prod[1])

        issue(0, even)

        def two(i, carry):
            issue(2 * i + 1, odd)
            d0 = finish(2 * i, even)
            flush(d0)
            issue(2 * i + 2, even)
            d1 = finish(2 * i + 1, odd)
            flush(d1)
            return carry

        lax.fori_loop(0, (steps + 1) // 2, two, 0)
        for m in range(2):
            pltpu.matmul_pop(even[m])

    acc = [pltpu.ACC(m)((TB, R), jnp.float32) for m in (0, 1, 0, 1, 0, 1)]
    pl.run_scoped(scoped, *acc)

    def out(a, carry):
        d = pl.ds(pl.multiple_of(a * TB, TB), TB)
        t = totals[d, :]
        low, high = t[:, :TB], t[:, TB:]
        keep_ref[d, :] = jnp.where(f == 0, low, high)
        give_ref[d, :] = jnp.where(f == 0, high, low).astype(jnp.bfloat16)
        weight_ref[pl.ds(a, 1), :] = jnp.sum(sums[d, :].T, axis=0, keepdims=True)
        return carry

    lax.fori_loop(0, UB, out, 0)


def combine_kernel(keep, give, weight, out, got, got_weight, send, recv):
    f, b = lax.axis_index("fiber"), lax.axis_index("blk")
    partner = {"fiber": 1 - f, "blk": b}
    barrier = pltpu.get_barrier_semaphore()
    pl.semaphore_signal(barrier, inc=1, device_id=partner, device_id_type=MESH)
    pl.semaphore_wait(barrier, 1)

    def copy(src, dst, n):
        return pltpu.make_async_remote_copy(
            src_ref=src,
            dst_ref=dst,
            send_sem=send.at[n],
            recv_sem=recv.at[n],
            device_id=partner,
            device_id_type=MESH,
        )

    copies = [copy(weight, got_weight, 0)]
    parts, step = 8, UB // 8
    for i in range(parts):
        d = pl.ds(i * step * TB, step * TB)
        copies.append(copy(give.at[d], got.at[d], i + 1))
    for c in copies:
        c.start()
    copies[0].wait_recv()
    scale = lax.rsqrt(1.0 + weight[...] + got_weight[...])
    for i in range(parts):
        copies[i + 1].wait_recv()
        for j in range(step):
            a = i * step + j
            d = pl.ds(a * TB, TB)
            by_row = jnp.broadcast_to(scale[a : a + 1, :], (TB, TB)).T
            out[d, :] = ((keep[d, :] + got[d, :].astype(jnp.float32)) * by_row).astype(jnp.bfloat16)
    for c in copies:
        c.wait_send()


def shards(users, items, tile_users, tile_items, confidence):
    vmem = pl.BlockSpec(memory_space=pltpu.VMEM)
    smem = pl.BlockSpec(memory_space=pltpu.SMEM)
    any_space = pl.BlockSpec(memory_space=pl.ANY)
    bf16, f32 = jnp.bfloat16, jnp.float32
    rows = UB * TB
    u_all, v_all, vt_all, c_all, perm = pl.pallas_call(
        gather_kernel,
        name="gather",
        in_specs=[any_space, any_space, any_space, vmem, vmem],
        out_specs=[vmem, vmem, vmem, vmem, vmem],
        out_shape=(
            pltpu.VMEM((2, rows, TB), bf16),
            pltpu.VMEM((IB, TB, R), bf16),
            pltpu.VMEM((IB, R, TB), bf16),
            pltpu.VMEM((T + 1, TB, TB), bf16),
            jax.ShapeDtypeStruct((8, SLOTS), jnp.int32),
        ),
        scratch_shapes=[
            pltpu.SemaphoreType.DMA((65,)),
            pltpu.SemaphoreType.DMA((65,)),
            pltpu.SemaphoreType.DMA((3,)),
        ],
        compiler_params=pltpu.CompilerParams(collective_id=0, has_side_effects=True, vmem_limit_bytes=8 << 20),
    )(
        users,
        items.reshape(2, TB, R),
        confidence.reshape(T, TB, TB),
        tile_users.reshape(1, T),
        tile_items.reshape(1, T),
    )
    keep, give, weight = pl.pallas_call(
        products_kernel,
        name="products",
        in_specs=[smem, vmem, vmem, vmem, vmem],
        out_specs=[vmem, vmem, vmem],
        out_shape=(
            pltpu.VMEM((rows, TB), f32),
            pltpu.VMEM((rows, TB), bf16),
            pltpu.VMEM((UB, TB), f32),
        ),
        scratch_shapes=[pltpu.VMEM((rows, R), f32), pltpu.VMEM((rows, TB), f32)],
        compiler_params=pltpu.CompilerParams(vmem_limit_bytes=12 << 20),
    )(perm, u_all, v_all, vt_all, c_all)
    return pl.pallas_call(
        combine_kernel,
        name="combine",
        in_specs=[vmem, vmem, vmem],
        out_specs=vmem,
        out_shape=jax.ShapeDtypeStruct((rows, TB), bf16),
        scratch_shapes=[
            pltpu.VMEM((rows, TB), bf16),
            pltpu.VMEM((UB, TB), f32),
            pltpu.SemaphoreType.DMA((9,)),
            pltpu.SemaphoreType.DMA((9,)),
        ],
        compiler_params=pltpu.CompilerParams(collective_id=1, has_side_effects=True, vmem_limit_bytes=8 << 20),
    )(keep, give, weight)


def solution(mesh):
    in_specs = (
        P("blk", "fiber"),
        P("blk", None),
        P("blk", "fiber", None),
        P("blk", "fiber", None),
        P("blk", "fiber", None, None, None),
    )

    def run(*args):
        with jax.sharding.use_abstract_mesh(mesh.abstract_mesh):
            return jax.shard_map(
                shards, mesh=mesh, in_specs=in_specs, out_specs=P("blk", "fiber"), check_vma=False
            )(*args)

    return run
```

```python
import functools

import jax
import jax.numpy as jnp
from jax import lax
from jax.experimental import pallas as pl
from jax.experimental.pallas import tpu as pltpu
from jax.sharding import PartitionSpec as P

MESH = pl.DeviceIdType.MESH
TB = 128
UB = 16
IB = 128
T = 512
R = 256
G = 4
DEEP, AHEAD, BEHIND = 4, 3, 2
NC = 4
CB = UB // NC
LAG = 6
SWAPS = 4
EXTRA = 16
SLOTS = 640

PLAN = (
    (0, 0, 0, 1, "M"), (0, 0, -1, 0, "P"), (1, 1, 0, 0, "A"), (0, 0, 0, -1, "P"), (0, 0, 1, 0, "M"),
    (0, 1, 0, 1, "M"), (0, 1, 0, -1, "P"), (1, 0, 0, 0, "A"), (0, 1, -1, 0, "P"), (0, 1, 1, 0, "M"),
    (0, 0, -1, 1, "p"), (0, 0, 0, 2, "M"), (1, 1, -1, 0, "A"), (0, 0, 1, 1, "m"), (0, 0, -1, -1, "P"),
    (0, 0, 2, 0, "P"), (1, 1, 1, 0, "M"), (1, 0, 0, 1, "A"), (1, 1, 0, -1, "P"), (0, 0, 1, -1, "m"),
    (0, 1, 1, 1, "m"), (1, 0, -1, 0, "P"), (0, 1, -1, 1, "F"), (1, 0, 0, -1, "A"), (0, 1, 1, -1, "m"),
    (0, 1, 2, 0, "P"), (1, 0, 1, 0, "M"), (0, 0, -1, 2, "P"), (0, 1, 0, 2, "F"), (1, 1, -1, 1, "A"),
    (0, 0, 1, 2, "M"), (0, 0, 2, -1, "p"), (0, 0, 2, 1, "M"), (1, 1, -1, -1, "p"), (0, 1, -1, -1, "F"),
    (1, 0, 1, 1, "m"), (1, 0, 2, 0, "P"), (1, 1, 1, 1, "A"), (1, 1, 1, -1, "m"), (1, 0, -1, -1, "P"),
    (1, 1, 0, 1, "F"), (0, 1, 2, 1, "p"), (0, 1, -1, 2, "M"), (1, 1, 2, 0, "A"), (1, 0, 1, -1, "m"),
    (0, 0, 2, 2, "p"), (0, 1, 1, 2, "m"), (0, 1, 2, -1, "p"), (1, 0, -1, 1, "A"), (1, 1, -1, 2, "M"),
    (1, 0, 2, -1, "P"), (1, 1, 2, 1, "m"), (1, 1, 1, 2, "P"), (1, 0, 0, 2, "A"), (1, 1, 2, -1, "m"),
    (1, 0, -1, 2, "P"), (1, 1, 0, 2, "M"), (1, 0, 1, 2, "P"), (1, 0, 2, 1, "A"), (0, 1, 2, 2, "M"),
    (1, 0, 2, 2, "P"), (1, 1, 2, 2, "m"),
)


def order_tiles(tu_ref, ti_ref, perm_ref):
    users = tu_ref[...]
    owner = lax.broadcasted_iota(jnp.int32, (UB, T), 0) == users
    hot = owner.astype(jnp.float32).astype(jnp.bfloat16)
    before = lax.broadcasted_iota(jnp.int32, (T, T), 0) < lax.broadcasted_iota(jnp.int32, (T, T), 1)
    rank = jnp.dot(hot, before.astype(jnp.float32).astype(jnp.bfloat16), preferred_element_type=jnp.float32)
    count = jnp.sum(owner.astype(jnp.float32), axis=1, keepdims=True)
    steps = jnp.floor((count + (G - 1)) * (1.0 / G))
    block = lax.broadcasted_iota(jnp.int32, (UB, 1), 0)
    lane = lax.broadcasted_iota(jnp.int32, (1, SLOTS), 1)
    start = jnp.zeros((UB, 1), jnp.float32)
    marks = jnp.zeros((1, SLOTS), jnp.float32)
    base = jnp.zeros((1, 1), jnp.float32)
    for c in range(NC):
        marks = marks + jnp.where(lane == c, base, 0.0)
        inside = base
        for a in range(c * CB, (c + 1) * CB):
            start = start + jnp.where(block == a, inside * G, 0.0)
            inside = inside + steps[a : a + 1, :]
        rounds = jnp.maximum(jnp.floor((inside - base + (DEEP - 1)) * (1.0 / DEEP)), 1.0)
        base = base + rounds * DEEP
    marks = marks + jnp.where(lane == NC, base, 0.0)
    place = jnp.sum(jnp.where(owner, rank + start, 0.0), axis=0, keepdims=True)
    match = lax.broadcasted_iota(jnp.int32, (SLOTS, T), 0) == place.astype(jnp.int32)
    number = lax.broadcasted_iota(jnp.int32, (1, T), 1) + 1
    rows = lax.broadcasted_iota(jnp.int32, (8, T), 0)
    fields = jnp.where(
        rows == 0,
        number // 256,
        jnp.where(rows == 1, number % 256, jnp.where(rows == 2, ti_ref[...], users)),
    )
    found = lax.dot_general(
        fields.astype(jnp.float32).astype(jnp.bfloat16),
        match.astype(jnp.float32).astype(jnp.bfloat16),
        (((1,), (1,)), ((), ())),
        preferred_element_type=jnp.float32,
    )
    packed = found[0:1] * (256.0 * 2048.0) + found[1:2] * 2048.0 + found[2:3] * 16.0 + found[3:4]
    out_rows = lax.broadcasted_iota(jnp.int32, (8, SLOTS), 0)
    perm_ref[...] = jnp.where(out_rows == 0, packed, marks).astype(jnp.int32)


def source(unit):
    z, h, dp, dq, via = unit
    if via == "A":
        return 0, 1 - h, dp, dq
    if via == "F":
        return z, 1 - h, dp, dq
    back = 1 if via in "Pp" else -1
    if dq and via in "PM":
        dq = (dq + back + 1) % 4 - 1
    else:
        dp = (dp + back + 1) % 4 - 1
    return z, h, dp, dq


def gather_kernel(users, items, conf, tile_users, tile_items, u_all, v_all, vt_all, c_all, perm, tu, ti, send, recv, local):
    f, b = lax.axis_index("fiber"), lax.axis_index("blk")
    zh, x, y, k = b // 32, (b // 8) % 4, (b // 2) % 4, b % 2
    p, q = x * (1 - k) + y * k, y * (1 - k) + x * k

    def shard(zh_, p_, q_, k_):
        return zh_ * 32 + (p_ * (1 - k_) + q_ * k_) * 8 + (q_ * (1 - k_) + p_ * k_) * 2 + k_

    def mine(z, h, dp, dq):
        return shard(zh if z == 0 else 1 - zh, (p + dp) % 4, (q + dq) % 4, k) * 2 + (f + h) % 2

    def others(z, h, dp, dq):
        return shard(zh if z == 0 else 1 - zh, (q + dp) % 4, (p + dq) % 4, 1 - k) * 2 + (f + h) % 2

    def dev(blk, fib=f):
        return {"fiber": fib, "blk": blk}

    first = {"P": dev(shard(zh, (p + 1) % 4, q, k)), "M": dev(shard(zh, (p + 3) % 4, q, k))}
    second = {"P": dev(shard(zh, p, (q + 1) % 4, k)), "M": dev(shard(zh, p, (q + 3) % 4, k))}
    across = dev(shard(1 - zh, p, q, k), 1 - f)
    sibling = dev(b + 1 - 2 * k)
    partner = dev(b, 1 - f)
    around = [first["P"], first["M"], second["P"], second["M"], across, sibling, partner]

    barrier = pltpu.get_barrier_semaphore()
    for d in around:
        pl.semaphore_signal(barrier, inc=1, device_id=d, device_id_type=MESH)
    pl.semaphore_wait(barrier, len(around))

    def slot(z, h, dp, dq):
        return z * 32 + h * 16 + (dp % 4) * 4 + dq % 4

    def copy(src, dst, n, d):
        return pltpu.make_async_remote_copy(
            src_ref=src, dst_ref=dst, send_sem=send.at[n], recv_sem=recv.at[n], device_id=d, device_id_type=MESH
        )

    def target(unit):
        dq, via = unit[3:]
        if via == "A":
            return across
        if via == "F":
            return partner
        return (second if dq and via in "PM" else first)[via.upper()]

    children = {}
    for unit in reversed(PLAN):
        children.setdefault(source(unit), []).append(unit)

    def weight(unit):
        return 1 + sum(weight(c[:4]) for c in children.get(unit, ()))

    sent = []

    def have(unit):
        n = mine(*unit)
        src = items.at[(f + unit[1]) % 2] if unit[0] == unit[2] == unit[3] == 0 else v_all.at[n]
        for c in sorted(children.get(unit, ()), key=lambda c: -weight(c[:4])):
            sent.append(copy(src, v_all.at[n], slot(*c[:4]), target(c)))
            sent[-1].start()
        sent.append(copy(src, v_all.at[n], slot(*unit) + 64, sibling))
        sent[-1].start()

    def turn(n):
        vt_all[n] = v_all[n].T

    swaps = []

    def swap(i):
        d = pl.ds(i * (UB * TB // SWAPS), UB * TB // SWAPS)
        swaps.append((copy(users.at[d], u_all.at[f, d], 128 + i, partner), copy(users.at[d], u_all.at[1 - f, d], 128 + i, partner)))
        swaps[-1][0].start()

    own = pltpu.make_async_copy(items, v_all.at[pl.ds(b * 2, 2)], local.at[0])
    half = pltpu.make_async_copy(users, u_all.at[f], local.at[1])
    tiles = pltpu.make_async_copy(conf, c_all.at[pl.ds(1, T)], local.at[2])
    lists = [
        pltpu.make_async_copy(tile_users, tu, local.at[3]),
        pltpu.make_async_copy(tile_items, ti, local.at[4]),
    ]
    for h in range(2):
        have((0, h, 0, 0))
    swap(0)
    own.start()
    for c in lists:
        c.start()
    half.start()
    tiles.start()
    c_all[0] = jnp.zeros((TB, TB), jnp.bfloat16)

    def own_work():
        own.wait()
        for j in range(2):
            turn(b * 2 + j)
        for c in lists:
            c.wait()
        order_tiles(tu, ti, perm)

    order = [u[:4] for u in PLAN]
    late = [(0, h, 0, 0) for h in range(2)] + order
    for i in range(len(order) + LAG):
        if i < len(order):
            unit = order[i]
            n = mine(*unit)
            copy(v_all.at[n], v_all.at[n], slot(*unit), sibling).wait_recv()
            have(unit)
            turn(n)
            if i == 30:
                own_work()
            if i % 8 == 7 and len(swaps) < SWAPS:
                swap(len(swaps))
        if i >= LAG - 2:
            unit = late[i - (LAG - 2)]
            n = others(*unit)
            copy(v_all.at[n], v_all.at[n], slot(*unit) + 64, sibling).wait_recv()
            turn(n)
    half.wait()
    tiles.wait()
    for out, into in swaps:
        into.wait_recv()
        out.wait_send()
    for c in sent:
        c.wait_send()


def products_kernel(chunk, perm, u_all, v_all, vt_all, c_all, keep_ref, give_ref, weight_ref, totals, sums):
    f = lax.axis_index("fiber")
    totals[...] = jnp.zeros_like(totals)
    sums[...] = jnp.zeros_like(sums)
    begin = perm[1, chunk]
    rounds = (perm[1, chunk + 1] - begin) // DEEP

    def entry(s, j):
        return perm[0, (begin + s) * G + j]

    def item(e):
        return lax.shift_right_logical(e, 4) & 127

    def rows(s, first=0):
        a = jnp.maximum((entry(s, 0) & 15) - first, 0)
        return pl.ds(pl.multiple_of(a * TB, TB), TB)

    def scoped(*accs):
        scores_acc = [(accs[2 * n], accs[2 * n + 1]) for n in range(DEEP)]
        prod_acc = [(accs[2 * n], accs[2 * n + 1]) for n in range(DEEP, 2 * DEEP)]

        def issue(s, r):
            d = rows(s)
            u = jnp.concatenate([u_all[0, d, :], u_all[1, d, :]], axis=1)
            for m in range(2):
                e0, e1 = entry(s, 2 * m), entry(s, 2 * m + 1)
                vt = jnp.concatenate([vt_all[item(e0)], vt_all[item(e1)]], axis=1)
                pltpu.matmul_push_rhs(vt, 0, m)
                pltpu.matmul_acc_lhs(scores_acc[r % DEEP][m], u, load_staged_rhs=0)

        def finish(s, r):
            d = rows(s, chunk * CB)
            entries = [entry(s, j) for j in range(G)]
            weight_sum = None
            for m in range(2):
                e0, e1 = entries[2 * m], entries[2 * m + 1]
                v = jnp.concatenate([v_all[item(e0)], v_all[item(e1)]], axis=0)
                pltpu.matmul_push_rhs(v, 1, m)
                scores = pltpu.matmul_pop(scores_acc[r % DEEP][m])
                c0 = c_all[lax.shift_right_logical(e0, 11)].astype(jnp.float32)
                c1 = c_all[lax.shift_right_logical(e1, 11)].astype(jnp.float32)
                weight = jnp.concatenate([c0, c1], axis=1) * (1.0 - scores)
                pltpu.matmul_acc_lhs(prod_acc[r % DEEP][m], weight.astype(jnp.bfloat16), load_staged_rhs=1)
                weight_sum = c0 + c1 if weight_sum is None else weight_sum + (c0 + c1)
            sums[d, :] += weight_sum

        def flush(s, r):
            low, high = prod_acc[r % DEEP]
            totals[rows(s, chunk * CB), :] += pltpu.matmul_pop(low) + pltpu.matmul_pop(high)

        def stage(s, r, first=False):
            issue(s + AHEAD, r + AHEAD)
            if not first:
                flush(s - BEHIND, r + DEEP - BEHIND)
            finish(s, r)

        for r in range(AHEAD):
            issue(r, r)
        for r in range(DEEP):
            stage(r, r, r < BEHIND)

        def several(i, carry):
            for r in range(DEEP):
                stage(i * DEEP + r, r)
            return carry

        lax.fori_loop(1, rounds, several, 0)
        for r in range(BEHIND):
            flush(rounds * DEEP - BEHIND + r, DEEP - BEHIND + r)
        for r in range(AHEAD):
            for m in range(2):
                pltpu.matmul_pop(scores_acc[r][m])

    pl.run_scoped(scoped, *[pltpu.ACC(n % 2)((TB, R), jnp.float32) for n in range(4 * DEEP)])

    sums_row = []
    for a in range(CB):
        d = pl.ds(a * TB, TB)
        t = totals[d, :]
        low, high = t[:, :TB], t[:, TB:]
        keep_ref[d, :] = jnp.where(f == 0, low, high)
        give_ref[d, :] = jnp.where(f == 0, high, low).astype(jnp.bfloat16)
        sums_row.append(jnp.sum(sums[d, :].T, axis=0, keepdims=True))
    weight = jnp.concatenate(sums_row, axis=0)
    weight_ref[...] = weight
    rest, parts = weight, []
    for _ in range(3):
        parts.append(rest.astype(jnp.bfloat16).astype(jnp.float32))
        rest = rest - parts[-1]
    parts.append(jnp.zeros((EXTRA - 3 * CB, TB), jnp.float32))
    give_ref[CB * TB :, :] = jnp.concatenate(parts, axis=0).astype(jnp.bfloat16)


def combine_kernel(*refs):
    out = refs[-1]
    for c in range(NC):
        keep, got, weight = refs[3 * c : 3 * c + 3]
        sent = got[CB * TB :, :].astype(jnp.float32)
        total = weight[...] + (sent[:CB] + (sent[CB : 2 * CB] + sent[2 * CB : 3 * CB]))
        scale = lax.rsqrt(1.0 + total)
        for a in range(CB):
            d = pl.ds(a * TB, TB)
            by_row = jnp.broadcast_to(scale[a : a + 1, :], (TB, TB)).T
            row = (keep[d, :] + got[d, :].astype(jnp.float32)) * by_row
            out[pl.ds((c * CB + a) * TB, TB), :] = row.astype(jnp.bfloat16)


def shards(users, items, tile_users, tile_items, confidence):
    vmem = pl.BlockSpec(memory_space=pltpu.VMEM)
    smem = pl.BlockSpec(memory_space=pltpu.SMEM)
    hbm = pl.BlockSpec(memory_space=pltpu.HBM)
    bf16, f32 = jnp.bfloat16, jnp.float32
    rows = UB * TB
    u_all, v_all, vt_all, c_all, perm = pl.pallas_call(
        gather_kernel,
        name="gather",
        in_specs=[hbm] * 5,
        out_specs=[vmem, vmem, vmem, vmem, vmem],
        out_shape=(
            pltpu.VMEM((2, rows, TB), bf16),
            pltpu.VMEM((IB, TB, R), bf16),
            pltpu.VMEM((IB, R, TB), bf16),
            pltpu.VMEM((T + 1, TB, TB), bf16),
            jax.ShapeDtypeStruct((8, SLOTS), jnp.int32),
        ),
        scratch_shapes=[
            pltpu.VMEM((1, T), jnp.int32),
            pltpu.VMEM((1, T), jnp.int32),
            pltpu.SemaphoreType.DMA((128 + SWAPS,)),
            pltpu.SemaphoreType.DMA((128 + SWAPS,)),
            pltpu.SemaphoreType.DMA((5,)),
        ],
        compiler_params=pltpu.CompilerParams(collective_id=0, has_side_effects=True, vmem_limit_bytes=8 << 20),
    )(
        *[
            pltpu.with_memory_space_constraint(z, pltpu.HBM)
            for z in (
                users,
                items.reshape(2, TB, R),
                confidence.reshape(T, TB, TB),
                tile_users.reshape(1, T),
                tile_items.reshape(1, T),
            )
        ]
    )
    tiles = T // NC
    parts = []
    for chunk in range(NC):
        keep, give, weight = pl.pallas_call(
            functools.partial(products_kernel, chunk),
            name="products",
            in_specs=[smem, vmem, vmem, vmem, vmem],
            out_specs=[vmem, vmem, vmem],
            out_shape=(
                pltpu.VMEM((CB * TB, TB), f32),
                pltpu.VMEM((CB * TB + EXTRA, TB), bf16),
                pltpu.VMEM((CB, TB), f32),
            ),
            scratch_shapes=[pltpu.VMEM((CB * TB, R), f32), pltpu.VMEM((CB * TB, TB), f32)],
            cost_estimate=pl.CostEstimate(
                flops=tiles * 4 * TB * TB * R, bytes_accessed=tiles * TB * TB * 8, transcendentals=0
            ),
            compiler_params=pltpu.CompilerParams(vmem_limit_bytes=8 << 20),
        )(perm, u_all, v_all, vt_all, c_all)
        parts += [keep, lax.ppermute(give, "fiber", [(0, 1), (1, 0)]), weight]
    return pl.pallas_call(
        combine_kernel,
        name="combine",
        in_specs=[vmem] * len(parts),
        out_specs=vmem,
        out_shape=jax.ShapeDtypeStruct((rows, TB), bf16),
        compiler_params=pltpu.CompilerParams(vmem_limit_bytes=8 << 20),
    )(*parts)


def solution(mesh):
    in_specs = (
        P("blk", "fiber"),
        P("blk", None),
        P("blk", "fiber", None),
        P("blk", "fiber", None),
        P("blk", "fiber", None, None, None),
    )

    def run(*args):
        with jax.sharding.use_abstract_mesh(mesh.abstract_mesh):
            return jax.shard_map(
                shards, mesh=mesh, in_specs=in_specs, out_specs=P("blk", "fiber"), check_vma=False
            )(*args)

    return run
```

```python
import functools

import jax
import jax.numpy as jnp
from jax import lax
from jax.experimental import pallas as pl
from jax.experimental.pallas import tpu as pltpu
from jax.sharding import PartitionSpec as P

MESH = pl.DeviceIdType.MESH
TB = 128
UB = 16
IB = 128
T = 512
R = 256
G = 4
DEEP, AHEAD, BEHIND = 4, 3, 2
CHUNKS = ((0, 7), (7, 13), (13, 16))
LAG = 6
SWAPS = 4
SLOTS = 640

PLAN = (
    (0, 0, 0, 1, "M"), (0, 0, -1, 0, "P"), (1, 1, 0, 0, "A"), (0, 0, 0, -1, "P"), (0, 0, 1, 0, "M"),
    (0, 1, 0, 1, "M"), (0, 1, 0, -1, "P"), (1, 0, 0, 0, "A"), (0, 1, -1, 0, "P"), (0, 1, 1, 0, "M"),
    (0, 0, -1, 1, "p"), (0, 0, 0, 2, "M"), (1, 1, -1, 0, "A"), (0, 0, 1, 1, "m"), (0, 0, -1, -1, "P"),
    (0, 0, 2, 0, "P"), (1, 1, 1, 0, "M"), (1, 0, 0, 1, "A"), (1, 1, 0, -1, "P"), (0, 0, 1, -1, "m"),
    (0, 1, 1, 1, "m"), (1, 0, -1, 0, "P"), (0, 1, -1, 1, "F"), (1, 0, 0, -1, "A"), (0, 1, 1, -1, "m"),
    (0, 1, 2, 0, "P"), (1, 0, 1, 0, "M"), (0, 0, -1, 2, "P"), (0, 1, 0, 2, "F"), (1, 1, -1, 1, "A"),
    (0, 0, 1, 2, "M"), (0, 0, 2, -1, "p"), (0, 0, 2, 1, "M"), (1, 1, -1, -1, "p"), (0, 1, -1, -1, "F"),
    (1, 0, 1, 1, "m"), (1, 0, 2, 0, "P"), (1, 1, 1, 1, "A"), (1, 1, 1, -1, "m"), (1, 0, -1, -1, "P"),
    (1, 1, 0, 1, "F"), (0, 1, 2, 1, "p"), (0, 1, -1, 2, "M"), (1, 1, 2, 0, "A"), (1, 0, 1, -1, "m"),
    (0, 0, 2, 2, "p"), (0, 1, 1, 2, "m"), (0, 1, 2, -1, "p"), (1, 0, -1, 1, "A"), (1, 1, -1, 2, "M"),
    (1, 0, 2, -1, "P"), (1, 1, 2, 1, "m"), (1, 1, 1, 2, "P"), (1, 0, 0, 2, "A"), (1, 1, 2, -1, "m"),
    (1, 0, -1, 2, "P"), (1, 1, 0, 2, "M"), (1, 0, 1, 2, "P"), (1, 0, 2, 1, "A"), (0, 1, 2, 2, "M"),
    (1, 0, 2, 2, "P"), (1, 1, 2, 2, "m"),
)


def order_tiles(tu_ref, ti_ref, perm_ref):
    users = tu_ref[...]
    owner = lax.broadcasted_iota(jnp.int32, (UB, T), 0) == users
    hot = owner.astype(jnp.float32).astype(jnp.bfloat16)
    before = lax.broadcasted_iota(jnp.int32, (T, T), 0) < lax.broadcasted_iota(jnp.int32, (T, T), 1)
    rank = jnp.dot(hot, before.astype(jnp.float32).astype(jnp.bfloat16), preferred_element_type=jnp.float32)
    count = jnp.sum(owner.astype(jnp.float32), axis=1, keepdims=True)
    steps = jnp.floor((count + (G - 1)) * (1.0 / G))
    block = lax.broadcasted_iota(jnp.int32, (UB, 1), 0)
    lane = lax.broadcasted_iota(jnp.int32, (1, SLOTS), 1)
    start = jnp.zeros((UB, 1), jnp.float32)
    marks = jnp.zeros((1, SLOTS), jnp.float32)
    base = jnp.zeros((1, 1), jnp.float32)
    for c, (low, high) in enumerate(CHUNKS):
        marks = marks + jnp.where(lane == c, base, 0.0)
        inside = base
        for a in range(low, high):
            start = start + jnp.where(block == a, inside * G, 0.0)
            inside = inside + steps[a : a + 1, :]
        rounds = jnp.maximum(jnp.floor((inside - base + (DEEP - 1)) * (1.0 / DEEP)), 1.0)
        base = base + rounds * DEEP
    marks = marks + jnp.where(lane == len(CHUNKS), base, 0.0)
    place = jnp.sum(jnp.where(owner, rank + start, 0.0), axis=0, keepdims=True)
    match = lax.broadcasted_iota(jnp.int32, (SLOTS, T), 0) == place.astype(jnp.int32)
    number = lax.broadcasted_iota(jnp.int32, (1, T), 1) + 1
    rows = lax.broadcasted_iota(jnp.int32, (8, T), 0)
    fields = jnp.where(
        rows == 0,
        number // 256,
        jnp.where(rows == 1, number % 256, jnp.where(rows == 2, ti_ref[...], users)),
    )
    found = lax.dot_general(
        fields.astype(jnp.float32).astype(jnp.bfloat16),
        match.astype(jnp.float32).astype(jnp.bfloat16),
        (((1,), (1,)), ((), ())),
        preferred_element_type=jnp.float32,
    )
    packed = found[0:1] * (256.0 * 2048.0) + found[1:2] * 2048.0 + found[2:3] * 16.0 + found[3:4]
    out_rows = lax.broadcasted_iota(jnp.int32, (8, SLOTS), 0)
    perm_ref[...] = jnp.where(out_rows == 0, packed, marks).astype(jnp.int32)


def source(unit):
    z, h, dp, dq, via = unit
    if via == "A":
        return 0, 1 - h, dp, dq
    if via == "F":
        return z, 1 - h, dp, dq
    back = 1 if via in "Pp" else -1
    if dq and via in "PM":
        dq = (dq + back + 1) % 4 - 1
    else:
        dp = (dp + back + 1) % 4 - 1
    return z, h, dp, dq


def gather_kernel(users, items, conf, tile_users, tile_items, u_all, v_all, vt_all, c_all, perm, tu, ti, send, recv, local):
    f, b = lax.axis_index("fiber"), lax.axis_index("blk")
    zh, x, y, k = b // 32, (b // 8) % 4, (b // 2) % 4, b % 2
    p, q = x * (1 - k) + y * k, y * (1 - k) + x * k

    def shard(zh_, p_, q_, k_):
        return zh_ * 32 + (p_ * (1 - k_) + q_ * k_) * 8 + (q_ * (1 - k_) + p_ * k_) * 2 + k_

    def mine(z, h, dp, dq):
        return shard(zh if z == 0 else 1 - zh, (p + dp) % 4, (q + dq) % 4, k) * 2 + (f + h) % 2

    def others(z, h, dp, dq):
        return shard(zh if z == 0 else 1 - zh, (q + dp) % 4, (p + dq) % 4, 1 - k) * 2 + (f + h) % 2

    def dev(blk, fib=f):
        return {"fiber": fib, "blk": blk}

    first = {"P": dev(shard(zh, (p + 1) % 4, q, k)), "M": dev(shard(zh, (p + 3) % 4, q, k))}
    second = {"P": dev(shard(zh, p, (q + 1) % 4, k)), "M": dev(shard(zh, p, (q + 3) % 4, k))}
    across = dev(shard(1 - zh, p, q, k), 1 - f)
    sibling = dev(b + 1 - 2 * k)
    partner = dev(b, 1 - f)
    around = [first["P"], first["M"], second["P"], second["M"], across, sibling, partner]

    barrier = pltpu.get_barrier_semaphore()
    for d in around:
        pl.semaphore_signal(barrier, inc=1, device_id=d, device_id_type=MESH)
    pl.semaphore_wait(barrier, len(around))

    def slot(z, h, dp, dq):
        return z * 32 + h * 16 + (dp % 4) * 4 + dq % 4

    def copy(src, dst, n, d):
        return pltpu.make_async_remote_copy(
            src_ref=src, dst_ref=dst, send_sem=send.at[n], recv_sem=recv.at[n], device_id=d, device_id_type=MESH
        )

    def target(unit):
        dq, via = unit[3:]
        if via == "A":
            return across
        if via == "F":
            return partner
        return (second if dq and via in "PM" else first)[via.upper()]

    children = {}
    for unit in reversed(PLAN):
        children.setdefault(source(unit), []).append(unit)

    def weight(unit):
        return 1 + sum(weight(c[:4]) for c in children.get(unit, ()))

    sent = []

    def have(unit):
        n = mine(*unit)
        src = items.at[(f + unit[1]) % 2] if unit[0] == unit[2] == unit[3] == 0 else v_all.at[n]
        for c in sorted(children.get(unit, ()), key=lambda c: -weight(c[:4])):
            sent.append(copy(src, v_all.at[n], slot(*c[:4]), target(c)))
            sent[-1].start()
        sent.append(copy(src, v_all.at[n], slot(*unit) + 64, sibling))
        sent[-1].start()

    def turn(n):
        vt_all[n] = v_all[n].T

    swaps = []

    def swap(i):
        d = pl.ds(i * (UB * TB // SWAPS), UB * TB // SWAPS)
        swaps.append((copy(users.at[d], u_all.at[f, d], 128 + i, partner), copy(users.at[d], u_all.at[1 - f, d], 128 + i, partner)))
        swaps[-1][0].start()

    own = pltpu.make_async_copy(items, v_all.at[pl.ds(b * 2, 2)], local.at[0])
    half = pltpu.make_async_copy(users, u_all.at[f], local.at[1])
    tiles = pltpu.make_async_copy(conf, c_all.at[pl.ds(1, T)], local.at[2])
    lists = [
        pltpu.make_async_copy(tile_users, tu, local.at[3]),
        pltpu.make_async_copy(tile_items, ti, local.at[4]),
    ]
    for h in range(2):
        have((0, h, 0, 0))
    swap(0)
    own.start()
    for c in lists:
        c.start()
    half.start()
    tiles.start()
    c_all[0] = jnp.zeros((TB, TB), jnp.bfloat16)

    def own_work():
        own.wait()
        for j in range(2):
            turn(b * 2 + j)
        for c in lists:
            c.wait()
        order_tiles(tu, ti, perm)

    order = [u[:4] for u in PLAN]
    late = [(0, h, 0, 0) for h in range(2)] + order
    for i in range(len(order) + LAG):
        if i < len(order):
            unit = order[i]
            n = mine(*unit)
            copy(v_all.at[n], v_all.at[n], slot(*unit), sibling).wait_recv()
            have(unit)
            turn(n)
            if i == 30:
                own_work()
            if i % 8 == 7 and len(swaps) < SWAPS:
                swap(len(swaps))
        if i >= LAG - 2:
            unit = late[i - (LAG - 2)]
            n = others(*unit)
            copy(v_all.at[n], v_all.at[n], slot(*unit) + 64, sibling).wait_recv()
            turn(n)
    half.wait()
    tiles.wait()
    for out, into in swaps:
        into.wait_recv()
        out.wait_send()
    for c in sent:
        c.wait_send()


def extra(blocks):
    return -(-3 * blocks // 16) * 16


def products_kernel(chunk, perm, u_all, v_all, vt_all, c_all, keep_ref, give_ref, weight_ref, totals, sums):
    f = lax.axis_index("fiber")
    start_block, end_block = CHUNKS[chunk]
    blocks = end_block - start_block
    totals[...] = jnp.zeros_like(totals)
    sums[...] = jnp.zeros_like(sums)
    begin = perm[1, chunk]
    rounds = (perm[1, chunk + 1] - begin) // DEEP

    def entry(s, j):
        return perm[0, (begin + s) * G + j]

    def item(e):
        return lax.shift_right_logical(e, 4) & 127

    def rows(s, first=0):
        a = jnp.maximum((entry(s, 0) & 15) - first, 0)
        return pl.ds(pl.multiple_of(a * TB, TB), TB)

    def scoped(*accs):
        scores_acc = [(accs[2 * n], accs[2 * n + 1]) for n in range(DEEP)]
        prod_acc = [(accs[2 * n], accs[2 * n + 1]) for n in range(DEEP, 2 * DEEP)]

        def issue(s, r):
            d = rows(s)
            u = jnp.concatenate([u_all[0, d, :], u_all[1, d, :]], axis=1)
            for m in range(2):
                e0, e1 = entry(s, 2 * m), entry(s, 2 * m + 1)
                vt = jnp.concatenate([vt_all[item(e0)], vt_all[item(e1)]], axis=1)
                pltpu.matmul_push_rhs(vt, 0, m)
                pltpu.matmul_acc_lhs(scores_acc[r % DEEP][m], u, load_staged_rhs=0)

        def finish(s, r):
            d = rows(s, start_block)
            entries = [entry(s, j) for j in range(G)]
            weight_sum = None
            for m in range(2):
                e0, e1 = entries[2 * m], entries[2 * m + 1]
                v = jnp.concatenate([v_all[item(e0)], v_all[item(e1)]], axis=0)
                pltpu.matmul_push_rhs(v, 1, m)
                scores = pltpu.matmul_pop(scores_acc[r % DEEP][m])
                c0 = c_all[lax.shift_right_logical(e0, 11)].astype(jnp.float32)
                c1 = c_all[lax.shift_right_logical(e1, 11)].astype(jnp.float32)
                weight = jnp.concatenate([c0, c1], axis=1) * (1.0 - scores)
                pltpu.matmul_acc_lhs(prod_acc[r % DEEP][m], weight.astype(jnp.bfloat16), load_staged_rhs=1)
                weight_sum = c0 + c1 if weight_sum is None else weight_sum + (c0 + c1)
            sums[d, :] += weight_sum

        def flush(s, r):
            low, high = prod_acc[r % DEEP]
            totals[rows(s, start_block), :] += pltpu.matmul_pop(low) + pltpu.matmul_pop(high)

        def stage(s, r, first=False):
            issue(s + AHEAD, r + AHEAD)
            if not first:
                flush(s - BEHIND, r + DEEP - BEHIND)
            finish(s, r)

        for r in range(AHEAD):
            issue(r, r)
        for r in range(DEEP):
            stage(r, r, r < BEHIND)

        def several(i, carry):
            for r in range(DEEP):
                stage(i * DEEP + r, r)
            return carry

        def twice(i, carry):
            return several(2 * i + 2, several(2 * i + 1, carry))

        lax.fori_loop(0, (rounds - 1) // 2, twice, 0)
        lax.fori_loop((rounds - 1) // 2 * 2 + 1, rounds, several, 0)
        for r in range(BEHIND):
            flush(rounds * DEEP - BEHIND + r, DEEP - BEHIND + r)
        for r in range(AHEAD):
            for m in range(2):
                pltpu.matmul_pop(scores_acc[r][m])

    pl.run_scoped(scoped, *[pltpu.ACC(n % 2)((TB, R), jnp.float32) for n in range(4 * DEEP)])

    sums_row = []
    for a in range(blocks):
        d = pl.ds(a * TB, TB)
        t = totals[d, :]
        low, high = t[:, :TB], t[:, TB:]
        keep_ref[d, :] = jnp.where(f == 0, low, high)
        give_ref[d, :] = jnp.where(f == 0, high, low).astype(jnp.bfloat16)
        sums_row.append(jnp.sum(sums[d, :].T, axis=0, keepdims=True))
    weight = jnp.concatenate(sums_row, axis=0)
    weight_ref[...] = weight
    rest, parts = weight, []
    for _ in range(3):
        parts.append(rest.astype(jnp.bfloat16).astype(jnp.float32))
        rest = rest - parts[-1]
    parts.append(jnp.zeros((extra(blocks) - 3 * blocks, TB), jnp.float32))
    give_ref[blocks * TB :, :] = jnp.concatenate(parts, axis=0).astype(jnp.bfloat16)


def combine_kernel(*refs):
    out = refs[-1]
    for c, (low, high) in enumerate(CHUNKS):
        n = high - low
        keep, got, weight = refs[3 * c : 3 * c + 3]
        sent = got[n * TB :, :].astype(jnp.float32)
        total = weight[...] + (sent[:n] + (sent[n : 2 * n] + sent[2 * n : 3 * n]))
        scale = lax.rsqrt(1.0 + total)
        for a in range(n):
            d = pl.ds(a * TB, TB)
            by_row = jnp.broadcast_to(scale[a : a + 1, :], (TB, TB)).T
            row = (keep[d, :] + got[d, :].astype(jnp.float32)) * by_row
            out[pl.ds((low + a) * TB, TB), :] = row.astype(jnp.bfloat16)


def shards(users, items, tile_users, tile_items, confidence):
    vmem = pl.BlockSpec(memory_space=pltpu.VMEM)
    smem = pl.BlockSpec(memory_space=pltpu.SMEM)
    hbm = pl.BlockSpec(memory_space=pltpu.HBM)
    bf16, f32 = jnp.bfloat16, jnp.float32
    rows = UB * TB
    u_all, v_all, vt_all, c_all, perm = pl.pallas_call(
        gather_kernel,
        name="gather",
        in_specs=[hbm] * 5,
        out_specs=[vmem, vmem, vmem, vmem, vmem],
        out_shape=(
            pltpu.VMEM((2, rows, TB), bf16),
            pltpu.VMEM((IB, TB, R), bf16),
            pltpu.VMEM((IB, R, TB), bf16),
            pltpu.VMEM((T + 1, TB, TB), bf16),
            jax.ShapeDtypeStruct((8, SLOTS), jnp.int32),
        ),
        scratch_shapes=[
            pltpu.VMEM((1, T), jnp.int32),
            pltpu.VMEM((1, T), jnp.int32),
            pltpu.SemaphoreType.DMA((128 + SWAPS,)),
            pltpu.SemaphoreType.DMA((128 + SWAPS,)),
            pltpu.SemaphoreType.DMA((5,)),
        ],
        compiler_params=pltpu.CompilerParams(collective_id=0, has_side_effects=True, vmem_limit_bytes=8 << 20),
    )(
        *[
            pltpu.with_memory_space_constraint(z, pltpu.HBM)
            for z in (
                users,
                items.reshape(2, TB, R),
                confidence.reshape(T, TB, TB),
                tile_users.reshape(1, T),
                tile_items.reshape(1, T),
            )
        ]
    )
    parts = []
    for chunk, (low, high) in enumerate(CHUNKS):
        n = high - low
        tiles = T * n // UB
        keep, give, weight = pl.pallas_call(
            functools.partial(products_kernel, chunk),
            name="products",
            in_specs=[smem, vmem, vmem, vmem, vmem],
            out_specs=[vmem, vmem, vmem],
            out_shape=(
                pltpu.VMEM((n * TB, TB), f32),
                pltpu.VMEM((n * TB + extra(n), TB), bf16),
                pltpu.VMEM((n, TB), f32),
            ),
            scratch_shapes=[pltpu.VMEM((n * TB, R), f32), pltpu.VMEM((n * TB, TB), f32)],
            cost_estimate=pl.CostEstimate(
                flops=tiles * 4 * TB * TB * R, bytes_accessed=tiles * TB * TB * 8, transcendentals=0
            ),
            compiler_params=pltpu.CompilerParams(vmem_limit_bytes=8 << 20),
        )(perm, u_all, v_all, vt_all, c_all)
        parts += [keep, lax.ppermute(give, "fiber", [(0, 1), (1, 0)]), weight]
    return pl.pallas_call(
        combine_kernel,
        name="combine",
        in_specs=[vmem] * len(parts),
        out_specs=vmem,
        out_shape=jax.ShapeDtypeStruct((rows, TB), bf16),
        compiler_params=pltpu.CompilerParams(vmem_limit_bytes=8 << 20),
    )(*parts)


def solution(mesh):
    in_specs = (
        P("blk", "fiber"),
        P("blk", None),
        P("blk", "fiber", None),
        P("blk", "fiber", None),
        P("blk", "fiber", None, None, None),
    )

    def run(*args):
        with jax.sharding.use_abstract_mesh(mesh.abstract_mesh):
            return jax.shard_map(
                shards, mesh=mesh, in_specs=in_specs, out_specs=P("blk", "fiber"), check_vma=False
            )(*args)

    return run
```

```python
import functools

import jax
import jax.numpy as jnp
from jax import lax
from jax.experimental import pallas as pl
from jax.experimental.pallas import tpu as pltpu
from jax.sharding import PartitionSpec as P

MESH = pl.DeviceIdType.MESH
TB = 128
UB = 16
IB = 128
T = 512
R = 256
G = 4
DEEP, AHEAD, BEHIND = 4, 3, 2
CHUNKS = ((0, 8), (8, 14), (14, 16))
LAG = 6
SWAPS = 4
SLOTS = 640

PLAN = (
    (0, 0, 1, 0, "M"), (0, 0, 0, -1, "P"), (0, 0, 0, 1, "M"), (0, 0, -1, 0, "P"), (1, 0, 0, 0, "A"),
    (0, 1, -1, 0, "P"), (0, 1, 0, 1, "M"), (0, 1, 0, -1, "P"), (0, 1, 1, 0, "M"), (0, 0, 1, -1, "P"),
    (0, 0, 1, 1, "M"), (0, 0, -1, -1, "p"), (1, 0, 0, 1, "M"), (1, 1, 1, 0, "A"), (0, 0, 0, 2, "P"),
    (1, 1, 0, 0, "F"), (1, 0, 1, 0, "M"), (0, 0, -1, 1, "p"), (1, 1, 0, 1, "A"), (0, 1, -1, 1, "M"),
    (0, 0, 2, 0, "P"), (0, 1, 1, 1, "m"), (1, 0, 0, -1, "P"), (1, 0, -1, 0, "A"), (0, 1, 0, 2, "M"),
    (0, 1, 2, 0, "P"), (0, 1, 1, -1, "m"), (0, 1, -1, -1, "P"), (0, 0, 2, 1, "m"), (1, 1, 1, -1, "A"),
    (1, 0, -1, 1, "p"), (1, 0, 0, 2, "M"), (1, 1, 1, 1, "M"), (1, 1, -1, 0, "P"), (1, 1, -1, -1, "A"),
    (0, 0, 1, 2, "m"), (1, 1, 0, -1, "P"), (0, 0, -1, 2, "M"), (0, 0, 2, -1, "P"), (0, 1, 1, 2, "M"),
    (1, 0, 1, 1, "A"), (1, 0, -1, -1, "p"), (1, 0, 1, -1, "m"), (0, 1, -1, 2, "p"), (0, 1, 2, -1, "P"),
    (0, 1, 2, 1, "M"), (1, 0, 2, 0, "A"), (1, 1, 2, -1, "m"), (1, 0, 2, 1, "p"), (1, 0, -1, 2, "M"),
    (1, 1, 2, 0, "P"), (1, 0, 1, 2, "m"), (1, 1, -1, 2, "P"), (1, 1, 1, 2, "M"), (1, 1, 0, 2, "P"),
    (1, 1, 2, 1, "m"), (0, 0, 2, 2, "p"), (1, 1, -1, 1, "M"), (1, 0, 2, -1, "p"), (0, 1, 2, 2, "m"),
    (1, 1, 2, 2, "P"), (1, 0, 2, 2, "M"),
)


def order_tiles(tu_ref, ti_ref, perm_ref):
    users = tu_ref[...]
    owner = lax.broadcasted_iota(jnp.int32, (UB, T), 0) == users
    hot = owner.astype(jnp.float32).astype(jnp.bfloat16)
    before = lax.broadcasted_iota(jnp.int32, (T, T), 0) < lax.broadcasted_iota(jnp.int32, (T, T), 1)
    rank = jnp.dot(hot, before.astype(jnp.float32).astype(jnp.bfloat16), preferred_element_type=jnp.float32)
    count = jnp.sum(owner.astype(jnp.float32), axis=1, keepdims=True)
    steps = jnp.floor((count + (G - 1)) * (1.0 / G))
    block = lax.broadcasted_iota(jnp.int32, (UB, 1), 0)
    lane = lax.broadcasted_iota(jnp.int32, (1, SLOTS), 1)
    start = jnp.zeros((UB, 1), jnp.float32)
    marks = jnp.zeros((1, SLOTS), jnp.float32)
    base = jnp.zeros((1, 1), jnp.float32)
    for c, (low, high) in enumerate(CHUNKS):
        marks = marks + jnp.where(lane == c, base, 0.0)
        inside = base
        for a in range(low, high):
            start = start + jnp.where(block == a, inside * G, 0.0)
            inside = inside + steps[a : a + 1, :]
        rounds = jnp.maximum(jnp.floor((inside - base + (DEEP - 1)) * (1.0 / DEEP)), 1.0)
        base = base + rounds * DEEP
    marks = marks + jnp.where(lane == len(CHUNKS), base, 0.0)
    place = jnp.sum(jnp.where(owner, rank + start, 0.0), axis=0, keepdims=True)
    match = lax.broadcasted_iota(jnp.int32, (SLOTS, T), 0) == place.astype(jnp.int32)
    number = lax.broadcasted_iota(jnp.int32, (1, T), 1) + 1
    rows = lax.broadcasted_iota(jnp.int32, (8, T), 0)
    fields = jnp.where(
        rows == 0,
        number // 256,
        jnp.where(rows == 1, number % 256, jnp.where(rows == 2, ti_ref[...], users)),
    )
    found = lax.dot_general(
        fields.astype(jnp.float32).astype(jnp.bfloat16),
        match.astype(jnp.float32).astype(jnp.bfloat16),
        (((1,), (1,)), ((), ())),
        preferred_element_type=jnp.float32,
    )
    packed = found[0:1] * (256.0 * 2048.0) + found[1:2] * 2048.0 + found[2:3] * 16.0 + found[3:4]
    out_rows = lax.broadcasted_iota(jnp.int32, (8, SLOTS), 0)
    perm_ref[...] = jnp.where(out_rows == 0, packed, marks).astype(jnp.int32)


def source(unit):
    z, h, dp, dq, via = unit
    if via == "A":
        return 0, 1 - h, dp, dq
    if via == "F":
        return z, 1 - h, dp, dq
    back = 1 if via in "Pp" else -1
    if dq and via in "PM":
        dq = (dq + back + 1) % 4 - 1
    else:
        dp = (dp + back + 1) % 4 - 1
    return z, h, dp, dq


def gather_kernel(users, items, conf, tile_users, tile_items, u_all, v_all, vt_all, c_all, perm, tu, ti, send, recv, local):
    f, b = lax.axis_index("fiber"), lax.axis_index("blk")
    zh, x, y, k = b // 32, (b // 8) % 4, (b // 2) % 4, b % 2
    p, q = x * (1 - k) + y * k, y * (1 - k) + x * k

    def shard(zh_, p_, q_, k_):
        return zh_ * 32 + (p_ * (1 - k_) + q_ * k_) * 8 + (q_ * (1 - k_) + p_ * k_) * 2 + k_

    def mine(z, h, dp, dq):
        return shard(zh if z == 0 else 1 - zh, (p + dp) % 4, (q + dq) % 4, k) * 2 + (f + h) % 2

    def others(z, h, dp, dq):
        return shard(zh if z == 0 else 1 - zh, (q + dp) % 4, (p + dq) % 4, 1 - k) * 2 + (f + h) % 2

    def dev(blk, fib=f):
        return {"fiber": fib, "blk": blk}

    first = {"P": dev(shard(zh, (p + 1) % 4, q, k)), "M": dev(shard(zh, (p + 3) % 4, q, k))}
    second = {"P": dev(shard(zh, p, (q + 1) % 4, k)), "M": dev(shard(zh, p, (q + 3) % 4, k))}
    across = dev(shard(1 - zh, p, q, k), 1 - f)
    sibling = dev(b + 1 - 2 * k)
    partner = dev(b, 1 - f)
    around = [first["P"], first["M"], second["P"], second["M"], across, sibling, partner]

    barrier = pltpu.get_barrier_semaphore()
    for d in around:
        pl.semaphore_signal(barrier, inc=1, device_id=d, device_id_type=MESH)
    pl.semaphore_wait(barrier, len(around))

    def slot(z, h, dp, dq):
        return z * 32 + h * 16 + (dp % 4) * 4 + dq % 4

    def copy(src, dst, n, d):
        return pltpu.make_async_remote_copy(
            src_ref=src, dst_ref=dst, send_sem=send.at[n], recv_sem=recv.at[n], device_id=d, device_id_type=MESH
        )

    def target(unit):
        dq, via = unit[3:]
        if via == "A":
            return across
        if via == "F":
            return partner
        return (second if dq and via in "PM" else first)[via.upper()]

    children = {}
    for unit in reversed(PLAN):
        children.setdefault(source(unit), []).append(unit)

    def weight(unit):
        return 1 + sum(weight(c[:4]) for c in children.get(unit, ()))

    sent = []

    def have(unit):
        n = mine(*unit)
        src = items.at[(f + unit[1]) % 2] if unit[0] == unit[2] == unit[3] == 0 else v_all.at[n]
        for c in sorted(children.get(unit, ()), key=lambda c: -weight(c[:4])):
            sent.append(copy(src, v_all.at[n], slot(*c[:4]), target(c)))
            sent[-1].start()
        sent.append(copy(src, v_all.at[n], slot(*unit) + 64, sibling))
        sent[-1].start()

    def turn(n):
        vt_all[n] = v_all[n].T

    swaps = []

    def swap(i):
        d = pl.ds(i * (UB * TB // SWAPS), UB * TB // SWAPS)
        swaps.append((copy(users.at[d], u_all.at[f, d], 128 + i, partner), copy(users.at[d], u_all.at[1 - f, d], 128 + i, partner)))
        swaps[-1][0].start()

    own = pltpu.make_async_copy(items, v_all.at[pl.ds(b * 2, 2)], local.at[0])
    half = pltpu.make_async_copy(users, u_all.at[f], local.at[1])
    tiles = pltpu.make_async_copy(conf, c_all.at[pl.ds(1, T)], local.at[2])
    lists = [
        pltpu.make_async_copy(tile_users, tu, local.at[3]),
        pltpu.make_async_copy(tile_items, ti, local.at[4]),
    ]
    for h in range(2):
        have((0, h, 0, 0))
    swap(0)
    own.start()
    for c in lists:
        c.start()
    half.start()
    tiles.start()
    c_all[0] = jnp.zeros((TB, TB), jnp.bfloat16)

    def own_work():
        own.wait()
        for j in range(2):
            turn(b * 2 + j)
        for c in lists:
            c.wait()
        order_tiles(tu, ti, perm)

    order = [u[:4] for u in PLAN]
    late = [(0, h, 0, 0) for h in range(2)] + order
    for i in range(len(order) + LAG):
        if i < len(order):
            unit = order[i]
            n = mine(*unit)
            copy(v_all.at[n], v_all.at[n], slot(*unit), sibling).wait_recv()
            have(unit)
            turn(n)
            if i == 30:
                own_work()
            if i % 8 == 7 and len(swaps) < SWAPS:
                swap(len(swaps))
        if i >= LAG - 2:
            unit = late[i - (LAG - 2)]
            n = others(*unit)
            copy(v_all.at[n], v_all.at[n], slot(*unit) + 64, sibling).wait_recv()
            turn(n)
    half.wait()
    tiles.wait()
    for out, into in swaps:
        into.wait_recv()
        out.wait_send()
    for c in sent:
        c.wait_send()


def extra(blocks):
    return -(-3 * blocks // 16) * 16


def products_kernel(chunk, perm, u_all, v_all, vt_all, c_all, keep_ref, give_ref, weight_ref, totals, sums):
    f = lax.axis_index("fiber")
    start_block, end_block = CHUNKS[chunk]
    blocks = end_block - start_block
    totals[...] = jnp.zeros_like(totals)
    sums[...] = jnp.zeros_like(sums)
    begin = perm[1, chunk]
    rounds = (perm[1, chunk + 1] - begin) // DEEP

    def entry(s, j):
        return perm[0, (begin + s) * G + j]

    def item(e):
        return lax.shift_right_logical(e, 4) & 127

    def rows(s, first=0):
        a = jnp.maximum((entry(s, 0) & 15) - first, 0)
        return pl.ds(pl.multiple_of(a * TB, TB), TB)

    def scoped(*accs):
        scores_acc = [(accs[2 * n], accs[2 * n + 1]) for n in range(DEEP)]
        prod_acc = [(accs[2 * n], accs[2 * n + 1]) for n in range(DEEP, 2 * DEEP)]

        def issue(s, r):
            d = rows(s)
            u = jnp.concatenate([u_all[0, d, :], u_all[1, d, :]], axis=1)
            for m in range(2):
                e0, e1 = entry(s, 2 * m), entry(s, 2 * m + 1)
                vt = jnp.concatenate([vt_all[item(e0)], vt_all[item(e1)]], axis=1)
                pltpu.matmul_push_rhs(vt, 0, m)
                pltpu.matmul_acc_lhs(scores_acc[r % DEEP][m], u, load_staged_rhs=0)

        def finish(s, r):
            d = rows(s, start_block)
            entries = [entry(s, j) for j in range(G)]
            weight_sum = None
            for m in range(2):
                e0, e1 = entries[2 * m], entries[2 * m + 1]
                v = jnp.concatenate([v_all[item(e0)], v_all[item(e1)]], axis=0)
                pltpu.matmul_push_rhs(v, 1, m)
                scores = pltpu.matmul_pop(scores_acc[r % DEEP][m])
                c0 = c_all[lax.shift_right_logical(e0, 11)].astype(jnp.float32)
                c1 = c_all[lax.shift_right_logical(e1, 11)].astype(jnp.float32)
                weight = jnp.concatenate([c0, c1], axis=1) * (1.0 - scores)
                pltpu.matmul_acc_lhs(prod_acc[r % DEEP][m], weight.astype(jnp.bfloat16), load_staged_rhs=1)
                weight_sum = c0 + c1 if weight_sum is None else weight_sum + (c0 + c1)
            sums[d, :] += weight_sum

        def flush(s, r):
            low, high = prod_acc[r % DEEP]
            totals[rows(s, start_block), :] += pltpu.matmul_pop(low) + pltpu.matmul_pop(high)

        def stage(s, r, first=False):
            issue(s + AHEAD, r + AHEAD)
            if not first:
                flush(s - BEHIND, r + DEEP - BEHIND)
            finish(s, r)

        for r in range(AHEAD):
            issue(r, r)
        for r in range(DEEP):
            stage(r, r, r < BEHIND)

        def several(i, carry):
            for r in range(DEEP):
                stage(i * DEEP + r, r)
            return carry

        def twice(i, carry):
            return several(2 * i + 2, several(2 * i + 1, carry))

        lax.fori_loop(0, (rounds - 1) // 2, twice, 0)
        lax.fori_loop((rounds - 1) // 2 * 2 + 1, rounds, several, 0)
        for r in range(BEHIND):
            flush(rounds * DEEP - BEHIND + r, DEEP - BEHIND + r)
        for r in range(AHEAD):
            for m in range(2):
                pltpu.matmul_pop(scores_acc[r][m])

    pl.run_scoped(scoped, *[pltpu.ACC(n % 2)((TB, R), jnp.float32) for n in range(4 * DEEP)])

    sums_row = []
    for a in range(blocks):
        d = pl.ds(a * TB, TB)
        t = totals[d, :]
        low, high = t[:, :TB], t[:, TB:]
        keep_ref[d, :] = jnp.where(f == 0, low, high)
        give_ref[d, :] = jnp.where(f == 0, high, low).astype(jnp.bfloat16)
        sums_row.append(jnp.sum(sums[d, :].T, axis=0, keepdims=True))
    weight = jnp.concatenate(sums_row, axis=0)
    weight_ref[...] = weight
    rest, parts = weight, []
    for _ in range(3):
        parts.append(rest.astype(jnp.bfloat16).astype(jnp.float32))
        rest = rest - parts[-1]
    parts.append(jnp.zeros((extra(blocks) - 3 * blocks, TB), jnp.float32))
    give_ref[blocks * TB :, :] = jnp.concatenate(parts, axis=0).astype(jnp.bfloat16)


def combine_kernel(*refs):
    out = refs[-1]
    for c, (low, high) in enumerate(CHUNKS):
        n = high - low
        keep, got, weight = refs[3 * c : 3 * c + 3]
        sent = got[n * TB :, :].astype(jnp.float32)
        total = weight[...] + (sent[:n] + (sent[n : 2 * n] + sent[2 * n : 3 * n]))
        scale = lax.rsqrt(1.0 + total)
        for a in range(n):
            d = pl.ds(a * TB, TB)
            by_row = jnp.broadcast_to(scale[a : a + 1, :], (TB, TB)).T
            row = (keep[d, :] + got[d, :].astype(jnp.float32)) * by_row
            out[pl.ds((low + a) * TB, TB), :] = row.astype(jnp.bfloat16)


def shards(users, items, tile_users, tile_items, confidence):
    vmem = pl.BlockSpec(memory_space=pltpu.VMEM)
    smem = pl.BlockSpec(memory_space=pltpu.SMEM)
    hbm = pl.BlockSpec(memory_space=pltpu.HBM)
    bf16, f32 = jnp.bfloat16, jnp.float32
    rows = UB * TB
    u_all, v_all, vt_all, c_all, perm = pl.pallas_call(
        gather_kernel,
        name="gather",
        in_specs=[hbm] * 5,
        out_specs=[vmem, vmem, vmem, vmem, vmem],
        out_shape=(
            pltpu.VMEM((2, rows, TB), bf16),
            pltpu.VMEM((IB, TB, R), bf16),
            pltpu.VMEM((IB, R, TB), bf16),
            pltpu.VMEM((T + 1, TB, TB), bf16),
            jax.ShapeDtypeStruct((8, SLOTS), jnp.int32),
        ),
        scratch_shapes=[
            pltpu.VMEM((1, T), jnp.int32),
            pltpu.VMEM((1, T), jnp.int32),
            pltpu.SemaphoreType.DMA((128 + SWAPS,)),
            pltpu.SemaphoreType.DMA((128 + SWAPS,)),
            pltpu.SemaphoreType.DMA((5,)),
        ],
        compiler_params=pltpu.CompilerParams(collective_id=0, has_side_effects=True, vmem_limit_bytes=8 << 20),
    )(
        *[
            pltpu.with_memory_space_constraint(z, pltpu.HBM)
            for z in (
                users,
                items.reshape(2, TB, R),
                confidence.reshape(T, TB, TB),
                tile_users.reshape(1, T),
                tile_items.reshape(1, T),
            )
        ]
    )
    parts = []
    for chunk, (low, high) in enumerate(CHUNKS):
        n = high - low
        tiles = T * n // UB
        keep, give, weight = pl.pallas_call(
            functools.partial(products_kernel, chunk),
            name="products",
            in_specs=[smem, vmem, vmem, vmem, vmem],
            out_specs=[vmem, vmem, vmem],
            out_shape=(
                pltpu.VMEM((n * TB, TB), f32),
                pltpu.VMEM((n * TB + extra(n), TB), bf16),
                pltpu.VMEM((n, TB), f32),
            ),
            scratch_shapes=[pltpu.VMEM((n * TB, R), f32), pltpu.VMEM((n * TB, TB), f32)],
            cost_estimate=pl.CostEstimate(
                flops=tiles * 4 * TB * TB * R, bytes_accessed=tiles * TB * TB * 8, transcendentals=0
            ),
            compiler_params=pltpu.CompilerParams(vmem_limit_bytes=8 << 20),
        )(perm, u_all, v_all, vt_all, c_all)
        parts += [keep, lax.ppermute(give, "fiber", [(0, 1), (1, 0)]), weight]
    return pl.pallas_call(
        combine_kernel,
        name="combine",
        in_specs=[vmem] * len(parts),
        out_specs=vmem,
        out_shape=jax.ShapeDtypeStruct((rows, TB), bf16),
        compiler_params=pltpu.CompilerParams(vmem_limit_bytes=8 << 20),
    )(*parts)


def solution(mesh):
    in_specs = (
        P("blk", "fiber"),
        P("blk", None),
        P("blk", "fiber", None),
        P("blk", "fiber", None),
        P("blk", "fiber", None, None, None),
    )

    def run(*args):
        with jax.sharding.use_abstract_mesh(mesh.abstract_mesh):
            return jax.shard_map(
                shards, mesh=mesh, in_specs=in_specs, out_specs=P("blk", "fiber"), check_vma=False
            )(*args)

    return run
```

```python
import functools

import jax
import jax.numpy as jnp
from jax import lax
from jax.experimental import pallas as pl
from jax.experimental.pallas import tpu as pltpu
from jax.sharding import PartitionSpec as P

MESH = pl.DeviceIdType.MESH
TB = 128
UB = 16
IB = 128
T = 512
R = 256
G = 4
DEEP, AHEAD, BEHIND = 4, 3, 2
CHUNKS = ((0, 8), (8, 13), (13, 16))
LAG = 6
SWAPS = 4
SLOTS = 640

PLAN = (
    (0, 0, 1, 0, "M"), (0, 0, -1, 0, "P"), (0, 0, 0, -1, "P"), (0, 0, 0, 1, "M"), (1, 0, 0, 0, "A"),
    (0, 1, 0, 1, "M"), (0, 1, -1, 0, "P"), (0, 1, 0, -1, "P"), (0, 1, 1, 0, "M"), (0, 0, 1, -1, "P"),
    (0, 0, 1, 1, "M"), (0, 0, 2, 0, "P"), (1, 0, 0, 1, "M"), (1, 1, 1, 0, "A"), (0, 0, -1, -1, "P"),
    (1, 0, 1, 0, "M"), (1, 1, 0, 0, "F"), (0, 0, 0, 2, "P"), (0, 1, 1, 1, "m"), (1, 1, -1, 0, "A"),
    (0, 0, -1, 1, "p"), (0, 1, 0, 2, "M"), (1, 1, 0, -1, "A"), (1, 0, 0, -1, "P"), (0, 1, -1, 1, "M"),
    (1, 0, -1, 0, "P"), (0, 0, 2, -1, "m"), (0, 1, 2, 0, "P"), (0, 1, 1, -1, "F"), (1, 1, 1, -1, "A"),
    (1, 0, 0, 2, "M"), (0, 1, -1, -1, "p"), (1, 1, 1, 1, "M"), (0, 0, 1, 2, "P"), (1, 1, 2, 0, "A"),
    (1, 1, 0, 1, "F"), (1, 0, 2, 0, "M"), (1, 0, -1, 1, "p"), (0, 1, 1, 2, "M"), (0, 0, 2, 1, "p"),
    (1, 0, 1, 1, "A"), (1, 1, -1, 1, "M"), (1, 1, 0, 2, "P"), (0, 0, -1, 2, "M"), (1, 1, -1, -1, "p"),
    (1, 1, 2, -1, "A"), (1, 0, 1, 2, "m"), (0, 1, 2, 1, "p"), (1, 1, 1, 2, "M"), (0, 1, 2, -1, "P"),
    (1, 0, 1, -1, "A"), (0, 0, 2, 2, "m"), (0, 1, -1, 2, "P"), (1, 0, -1, 2, "M"), (1, 0, 2, -1, "P"),
    (1, 0, -1, -1, "A"), (0, 1, 2, 2, "m"), (1, 0, 2, 1, "p"), (1, 1, -1, 2, "M"), (1, 1, 2, 1, "p"),
    (1, 0, 2, 2, "m"), (1, 1, 2, 2, "P"),
)


def order_tiles(tu_ref, ti_ref, perm_ref):
    users = tu_ref[...]
    owner = lax.broadcasted_iota(jnp.int32, (UB, T), 0) == users
    hot = owner.astype(jnp.float32).astype(jnp.bfloat16)
    before = lax.broadcasted_iota(jnp.int32, (T, T), 0) < lax.broadcasted_iota(jnp.int32, (T, T), 1)
    rank = jnp.dot(hot, before.astype(jnp.float32).astype(jnp.bfloat16), preferred_element_type=jnp.float32)
    count = jnp.sum(owner.astype(jnp.float32), axis=1, keepdims=True)
    steps = jnp.floor((count + (G - 1)) * (1.0 / G))
    block = lax.broadcasted_iota(jnp.int32, (UB, 1), 0)
    lane = lax.broadcasted_iota(jnp.int32, (1, SLOTS), 1)
    start = jnp.zeros((UB, 1), jnp.float32)
    marks = jnp.zeros((1, SLOTS), jnp.float32)
    base = jnp.zeros((1, 1), jnp.float32)
    for c, (low, high) in enumerate(CHUNKS):
        marks = marks + jnp.where(lane == c, base, 0.0)
        inside = base
        for a in range(low, high):
            start = start + jnp.where(block == a, inside * G, 0.0)
            inside = inside + steps[a : a + 1, :]
        rounds = jnp.maximum(jnp.floor((inside - base + (DEEP - 1)) * (1.0 / DEEP)), 1.0)
        base = base + rounds * DEEP
    marks = marks + jnp.where(lane == len(CHUNKS), base, 0.0)
    place = jnp.sum(jnp.where(owner, rank + start, 0.0), axis=0, keepdims=True)
    match = lax.broadcasted_iota(jnp.int32, (SLOTS, T), 0) == place.astype(jnp.int32)
    number = lax.broadcasted_iota(jnp.int32, (1, T), 1) + 1
    rows = lax.broadcasted_iota(jnp.int32, (8, T), 0)
    fields = jnp.where(
        rows == 0,
        number // 256,
        jnp.where(rows == 1, number % 256, jnp.where(rows == 2, ti_ref[...], users)),
    )
    found = lax.dot_general(
        fields.astype(jnp.float32).astype(jnp.bfloat16),
        match.astype(jnp.float32).astype(jnp.bfloat16),
        (((1,), (1,)), ((), ())),
        preferred_element_type=jnp.float32,
    )
    packed = found[0:1] * (256.0 * 2048.0) + found[1:2] * 2048.0 + found[2:3] * 16.0 + found[3:4]
    out_rows = lax.broadcasted_iota(jnp.int32, (8, SLOTS), 0)
    perm_ref[...] = jnp.where(out_rows == 0, packed, marks).astype(jnp.int32)


def source(unit):
    z, h, dp, dq, via = unit
    if via == "A":
        return 0, 1 - h, dp, dq
    if via == "F":
        return z, 1 - h, dp, dq
    back = 1 if via in "Pp" else -1
    if dq and via in "PM":
        dq = (dq + back + 1) % 4 - 1
    else:
        dp = (dp + back + 1) % 4 - 1
    return z, h, dp, dq


def gather_kernel(users, items, conf, tile_users, tile_items, u_all, v_all, vt_all, c_all, perm, tu, ti, send, recv, local):
    f, b = lax.axis_index("fiber"), lax.axis_index("blk")
    zh, x, y, k = b // 32, (b // 8) % 4, (b // 2) % 4, b % 2
    p, q = x * (1 - k) + y * k, y * (1 - k) + x * k

    def shard(zh_, p_, q_, k_):
        return zh_ * 32 + (p_ * (1 - k_) + q_ * k_) * 8 + (q_ * (1 - k_) + p_ * k_) * 2 + k_

    def mine(z, h, dp, dq):
        return shard(zh if z == 0 else 1 - zh, (p + dp) % 4, (q + dq) % 4, k) * 2 + (f + h) % 2

    def others(z, h, dp, dq):
        return shard(zh if z == 0 else 1 - zh, (q + dp) % 4, (p + dq) % 4, 1 - k) * 2 + (f + h) % 2

    def dev(blk, fib=f):
        return {"fiber": fib, "blk": blk}

    first = {"P": dev(shard(zh, (p + 1) % 4, q, k)), "M": dev(shard(zh, (p + 3) % 4, q, k))}
    second = {"P": dev(shard(zh, p, (q + 1) % 4, k)), "M": dev(shard(zh, p, (q + 3) % 4, k))}
    across = dev(shard(1 - zh, p, q, k), 1 - f)
    sibling = dev(b + 1 - 2 * k)
    partner = dev(b, 1 - f)
    around = [first["P"], first["M"], second["P"], second["M"], across, sibling, partner]

    barrier = pltpu.get_barrier_semaphore()
    for d in around:
        pl.semaphore_signal(barrier, inc=1, device_id=d, device_id_type=MESH)
    pl.semaphore_wait(barrier, len(around))

    def slot(z, h, dp, dq):
        return z * 32 + h * 16 + (dp % 4) * 4 + dq % 4

    def copy(src, dst, n, d):
        return pltpu.make_async_remote_copy(
            src_ref=src, dst_ref=dst, send_sem=send.at[n], recv_sem=recv.at[n], device_id=d, device_id_type=MESH
        )

    def target(unit):
        dq, via = unit[3:]
        if via == "A":
            return across
        if via == "F":
            return partner
        return (second if dq and via in "PM" else first)[via.upper()]

    children = {}
    for unit in reversed(PLAN):
        children.setdefault(source(unit), []).append(unit)

    def weight(unit):
        return 1 + sum(weight(c[:4]) for c in children.get(unit, ()))

    sent = []

    def have(unit):
        n = mine(*unit)
        src = items.at[(f + unit[1]) % 2] if unit[0] == unit[2] == unit[3] == 0 else v_all.at[n]
        for c in sorted(children.get(unit, ()), key=lambda c: -weight(c[:4])):
            sent.append(copy(src, v_all.at[n], slot(*c[:4]), target(c)))
            sent[-1].start()
        sent.append(copy(src, v_all.at[n], slot(*unit) + 64, sibling))
        sent[-1].start()

    def turn(n):
        vt_all[n] = v_all[n].T

    swaps = []

    def swap(i):
        d = pl.ds(i * (UB * TB // SWAPS), UB * TB // SWAPS)
        swaps.append((copy(users.at[d], u_all.at[f, d], 128 + i, partner), copy(users.at[d], u_all.at[1 - f, d], 128 + i, partner)))
        swaps[-1][0].start()

    own = pltpu.make_async_copy(items, v_all.at[pl.ds(b * 2, 2)], local.at[0])
    half = pltpu.make_async_copy(users, u_all.at[f], local.at[1])
    tiles = pltpu.make_async_copy(conf, c_all.at[pl.ds(1, T)], local.at[2])
    lists = [
        pltpu.make_async_copy(tile_users, tu, local.at[3]),
        pltpu.make_async_copy(tile_items, ti, local.at[4]),
    ]
    for h in range(2):
        have((0, h, 0, 0))
    swap(0)
    own.start()
    for c in lists:
        c.start()
    half.start()
    tiles.start()
    c_all[0] = jnp.zeros((TB, TB), jnp.bfloat16)

    def own_work():
        own.wait()
        for j in range(2):
            turn(b * 2 + j)
        for c in lists:
            c.wait()
        order_tiles(tu, ti, perm)

    order = [u[:4] for u in PLAN]
    late = [(0, h, 0, 0) for h in range(2)] + order
    for i in range(len(order) + LAG):
        if i < len(order):
            unit = order[i]
            n = mine(*unit)
            copy(v_all.at[n], v_all.at[n], slot(*unit), sibling).wait_recv()
            have(unit)
            turn(n)
            if i == 30:
                own_work()
            if i % 8 == 7 and len(swaps) < SWAPS:
                swap(len(swaps))
        if i >= LAG - 2:
            unit = late[i - (LAG - 2)]
            n = others(*unit)
            copy(v_all.at[n], v_all.at[n], slot(*unit) + 64, sibling).wait_recv()
            turn(n)
    half.wait()
    tiles.wait()
    for out, into in swaps:
        into.wait_recv()
        out.wait_send()
    for c in sent:
        c.wait_send()


def extra(blocks):
    return -(-3 * blocks // 16) * 16


def products_kernel(chunk, perm, u_all, v_all, vt_all, c_all, keep_ref, give_ref, weight_ref, totals, sums):
    f = lax.axis_index("fiber")
    start_block, end_block = CHUNKS[chunk]
    blocks = end_block - start_block
    totals[...] = jnp.zeros_like(totals)
    sums[...] = jnp.zeros_like(sums)
    begin = perm[1, chunk]
    rounds = (perm[1, chunk + 1] - begin) // DEEP

    def entry(s, j):
        return perm[0, (begin + s) * G + j]

    def item(e):
        return lax.shift_right_logical(e, 4) & 127

    def rows(s, first=0):
        a = jnp.maximum((entry(s, 0) & 15) - first, 0)
        return pl.ds(pl.multiple_of(a * TB, TB), TB)

    def scoped(*accs):
        scores_acc = [(accs[2 * n], accs[2 * n + 1]) for n in range(DEEP)]
        prod_acc = [(accs[2 * n], accs[2 * n + 1]) for n in range(DEEP, 2 * DEEP)]

        def issue(s, r):
            d = rows(s)
            u = jnp.concatenate([u_all[0, d, :], u_all[1, d, :]], axis=1)
            for m in range(2):
                e0, e1 = entry(s, 2 * m), entry(s, 2 * m + 1)
                vt = jnp.concatenate([vt_all[item(e0)], vt_all[item(e1)]], axis=1)
                pltpu.matmul_push_rhs(vt, 0, m)
                pltpu.matmul_acc_lhs(scores_acc[r % DEEP][m], u, load_staged_rhs=0)

        def finish(s, r):
            d = rows(s, start_block)
            entries = [entry(s, j) for j in range(G)]
            weight_sum = None
            for m in range(2):
                e0, e1 = entries[2 * m], entries[2 * m + 1]
                v = jnp.concatenate([v_all[item(e0)], v_all[item(e1)]], axis=0)
                pltpu.matmul_push_rhs(v, 1, m)
                scores = pltpu.matmul_pop(scores_acc[r % DEEP][m])
                c0 = c_all[lax.shift_right_logical(e0, 11)].astype(jnp.float32)
                c1 = c_all[lax.shift_right_logical(e1, 11)].astype(jnp.float32)
                weight = jnp.concatenate([c0, c1], axis=1) * (1.0 - scores)
                pltpu.matmul_acc_lhs(prod_acc[r % DEEP][m], weight.astype(jnp.bfloat16), load_staged_rhs=1)
                weight_sum = c0 + c1 if weight_sum is None else weight_sum + (c0 + c1)
            sums[d, :] += weight_sum

        def flush(s, r):
            low, high = prod_acc[r % DEEP]
            totals[rows(s, start_block), :] += pltpu.matmul_pop(low) + pltpu.matmul_pop(high)

        def stage(s, r, first=False):
            issue(s + AHEAD, r + AHEAD)
            if not first:
                flush(s - BEHIND, r + DEEP - BEHIND)
            finish(s, r)

        for r in range(AHEAD):
            issue(r, r)
        for r in range(DEEP):
            stage(r, r, r < BEHIND)

        def several(i, carry):
            for r in range(DEEP):
                stage(i * DEEP + r, r)
            return carry

        def twice(i, carry):
            return several(2 * i + 2, several(2 * i + 1, carry))

        lax.fori_loop(0, (rounds - 1) // 2, twice, 0)
        lax.fori_loop((rounds - 1) // 2 * 2 + 1, rounds, several, 0)
        for r in range(BEHIND):
            flush(rounds * DEEP - BEHIND + r, DEEP - BEHIND + r)
        for r in range(AHEAD):
            for m in range(2):
                pltpu.matmul_pop(scores_acc[r][m])

    pl.run_scoped(scoped, *[pltpu.ACC(n % 2)((TB, R), jnp.float32) for n in range(4 * DEEP)])

    sums_row = []
    for a in range(blocks):
        d = pl.ds(a * TB, TB)
        t = totals[d, :]
        low, high = t[:, :TB], t[:, TB:]
        keep_ref[d, :] = jnp.where(f == 0, low, high)
        give_ref[d, :] = jnp.where(f == 0, high, low).astype(jnp.bfloat16)
        sums_row.append(jnp.sum(sums[d, :].T, axis=0, keepdims=True))
    weight = jnp.concatenate(sums_row, axis=0)
    weight_ref[...] = weight
    rest, parts = weight, []
    for _ in range(3):
        parts.append(rest.astype(jnp.bfloat16).astype(jnp.float32))
        rest = rest - parts[-1]
    parts.append(jnp.zeros((extra(blocks) - 3 * blocks, TB), jnp.float32))
    give_ref[blocks * TB :, :] = jnp.concatenate(parts, axis=0).astype(jnp.bfloat16)


def combine_kernel(chunks, *refs):
    out, made, done = refs[-3:]
    base = chunks[0][0] * TB
    for c, (low, high) in enumerate(chunks):
        n = high - low
        keep, got, weight = refs[3 * c : 3 * c + 3]
        sent = got[n * TB :, :].astype(jnp.float32)
        total = weight[...] + (sent[:n] + (sent[n : 2 * n] + sent[2 * n : 3 * n]))
        scale = lax.rsqrt(1.0 + total)
        for a in range(n):
            d = pl.ds(a * TB, TB)
            by_row = jnp.broadcast_to(scale[a : a + 1, :], (TB, TB)).T
            row = (keep[d, :] + got[d, :].astype(jnp.float32)) * by_row
            made[pl.ds((low + a) * TB - base, TB), :] = row.astype(jnp.bfloat16)
    copy = pltpu.make_async_copy(made, out.at[pl.ds(base, made.shape[0])], done)
    copy.start()
    copy.wait()


def shards(users, items, tile_users, tile_items, confidence):
    vmem = pl.BlockSpec(memory_space=pltpu.VMEM)
    smem = pl.BlockSpec(memory_space=pltpu.SMEM)
    hbm = pl.BlockSpec(memory_space=pltpu.HBM)
    bf16, f32 = jnp.bfloat16, jnp.float32
    rows = UB * TB
    u_all, v_all, vt_all, c_all, perm = pl.pallas_call(
        gather_kernel,
        name="gather",
        in_specs=[hbm] * 5,
        out_specs=[vmem, vmem, vmem, vmem, vmem],
        out_shape=(
            pltpu.VMEM((2, rows, TB), bf16),
            pltpu.VMEM((IB, TB, R), bf16),
            pltpu.VMEM((IB, R, TB), bf16),
            pltpu.VMEM((T + 1, TB, TB), bf16),
            jax.ShapeDtypeStruct((8, SLOTS), jnp.int32),
        ),
        scratch_shapes=[
            pltpu.VMEM((1, T), jnp.int32),
            pltpu.VMEM((1, T), jnp.int32),
            pltpu.SemaphoreType.DMA((128 + SWAPS,)),
            pltpu.SemaphoreType.DMA((128 + SWAPS,)),
            pltpu.SemaphoreType.DMA((5,)),
        ],
        compiler_params=pltpu.CompilerParams(collective_id=0, has_side_effects=True, vmem_limit_bytes=8 << 20),
    )(
        *[
            pltpu.with_memory_space_constraint(z, pltpu.HBM)
            for z in (
                users,
                items.reshape(2, TB, R),
                confidence.reshape(T, TB, TB),
                tile_users.reshape(1, T),
                tile_items.reshape(1, T),
            )
        ]
    )
    parts = []
    for chunk, (low, high) in enumerate(CHUNKS):
        n = high - low
        tiles = T * n // UB
        keep, give, weight = pl.pallas_call(
            functools.partial(products_kernel, chunk),
            name="products",
            in_specs=[smem, vmem, vmem, vmem, vmem],
            out_specs=[vmem, vmem, vmem],
            out_shape=(
                pltpu.VMEM((n * TB, TB), f32),
                pltpu.VMEM((n * TB + extra(n), TB), bf16),
                pltpu.VMEM((n, TB), f32),
            ),
            scratch_shapes=[pltpu.VMEM((n * TB, R), f32), pltpu.VMEM((n * TB, TB), f32)],
            cost_estimate=pl.CostEstimate(
                flops=tiles * 4 * TB * TB * R, bytes_accessed=tiles * TB * TB * 8, transcendentals=0
            ),
            compiler_params=pltpu.CompilerParams(vmem_limit_bytes=8 << 20),
        )(perm, u_all, v_all, vt_all, c_all)
        parts += [keep, lax.ppermute(give, "fiber", [(0, 1), (1, 0)]), weight]
    out = None
    for chunks in (CHUNKS[:-1], CHUNKS[-1:]):
        own, parts = parts[: 3 * len(chunks)], parts[3 * len(chunks) :]
        count = chunks[-1][1] - chunks[0][0]
        before = [] if out is None else [out]
        out = pl.pallas_call(
            functools.partial(combine_kernel, chunks),
            name="combine",
            in_specs=[vmem] * len(own) + [hbm] * len(before),
            out_specs=hbm,
            out_shape=jax.ShapeDtypeStruct((rows, TB), bf16),
            input_output_aliases={len(own): 0} if before else {},
            scratch_shapes=[pltpu.VMEM((count * TB, TB), bf16), pltpu.SemaphoreType.DMA],
            cost_estimate=pl.CostEstimate(flops=count * TB * TB * 4, bytes_accessed=count * TB * TB * 10, transcendentals=0),
            compiler_params=pltpu.CompilerParams(vmem_limit_bytes=8 << 20),
        )(*own, *before)
    return out


def solution(mesh):
    in_specs = (
        P("blk", "fiber"),
        P("blk", None),
        P("blk", "fiber", None),
        P("blk", "fiber", None),
        P("blk", "fiber", None, None, None),
    )

    def run(*args):
        with jax.sharding.use_abstract_mesh(mesh.abstract_mesh):
            return jax.shard_map(
                shards, mesh=mesh, in_specs=in_specs, out_specs=P("blk", "fiber"), check_vma=False
            )(*args)

    return run
```
